32 devices in a mesh: fsdp: 8 (over y, x, core), sp: 4 (over z).
Axes of the slice: x: 2, y: 2, z: 4, core: 2. Of those that a mesh axis runs over, the one named last changes fastest.
Arguments:
- tokens: bfloat16 [5120, 1536], P(('fsdp', 'sp')), may hold values from -6 to 6
- condition: bfloat16 [32, 1536], P('fsdp'), may hold values from -6 to 6
- caption: bfloat16 [4096, 4096], P(('fsdp', 'sp')), may hold values from -6 to 6
- clip_lengths: int32 [8, 4], P('fsdp'), may hold values from 0 to 640, as said below
- caption_lengths: int32 [32], P('fsdp'), may hold values from 1 to 128, as said below
- positions: int32 [5120], P(('fsdp', 'sp')), may hold values from 0 to 639, as said below
- ada_weight: bfloat16 [1536, 9216], P(('fsdp', 'sp')), may hold values from -0.15625 to 0.15625
- ada_bias: bfloat16 [9216], P(('fsdp', 'sp')), may hold values from -3 to 3
- attention_gain: bfloat16 [1536], P(('fsdp', 'sp')), may hold values from 0.5 to 1.5
- qkv_weight: bfloat16 [1536, 4608], P(('fsdp', 'sp')), may hold values from -0.15625 to 0.15625
- query_gain: bfloat16 [1536], P(('fsdp', 'sp')), may hold values from 0.5 to 1.5
- key_gain: bfloat16 [1536], P(('fsdp', 'sp')), may hold values from 0.5 to 1.5
- text_key_weight: bfloat16 [4096, 1536], P(('fsdp', 'sp')), may hold values from -0.09375 to 0.09375
- text_key_gain: bfloat16 [1536], P(('fsdp', 'sp')), may hold values from 0.5 to 1.5
- text_value_weight: bfloat16 [4096, 1536], P(('fsdp', 'sp')), may hold values from -0.09375 to 0.09375
- cross_gate: bfloat16 [1536], P(('fsdp', 'sp')), may hold values from -3 to 3
- out_weight: bfloat16 [1536, 1536], P(('fsdp', 'sp')), may hold values from -5 to 5
- feedforward_gain: bfloat16 [1536], P(('fsdp', 'sp')), may hold values from 0.5 to 1.5
- gate_weight: bfloat16 [1536, 4096], P(('fsdp', 'sp')), may hold values from -0.15625 to 0.15625
- up_weight: bfloat16 [1536, 4096], P(('fsdp', 'sp')), may hold values from -0.15625 to 0.15625
- down_weight: bfloat16 [4096, 1536], P(('fsdp', 'sp')), may hold values from -0.09375 to 0.09375
- out_grad: bfloat16 [5120, 1536], P(('fsdp', 'sp')), may hold values from -6 to 6
Outputs:
- output: bfloat16 [5120, 1536], P(('fsdp', 'sp'))
- tokens_grad: float32 [5120, 1536], P(('fsdp', 'sp'))
- ada_weight_grad: float32 [1536, 9216], P(('fsdp', 'sp'))
- ada_bias_grad: float32 [9216], P(('fsdp', 'sp'))
- attention_gain_grad: float32 [1536], P(('fsdp', 'sp'))
- qkv_weight_grad: float32 [1536, 4608], P(('fsdp', 'sp'))
- query_gain_grad: float32 [1536], P(('fsdp', 'sp'))
- key_gain_grad: float32 [1536], P(('fsdp', 'sp'))
- text_key_weight_grad: float32 [4096, 1536], P(('fsdp', 'sp'))
- text_key_gain_grad: float32 [1536], P(('fsdp', 'sp'))
- text_value_weight_grad: float32 [4096, 1536], P(('fsdp', 'sp'))
- cross_gate_grad: float32 [1536], P(('fsdp', 'sp'))
- out_weight_grad: float32 [1536, 1536], P(('fsdp', 'sp'))
- feedforward_gain_grad: float32 [1536], P(('fsdp', 'sp'))
- gate_weight_grad: float32 [1536, 4096], P(('fsdp', 'sp'))
- up_weight_grad: float32 [1536, 4096], P(('fsdp', 'sp'))
- down_weight_grad: float32 [4096, 1536], P(('fsdp', 'sp'))
The draws below stay inside these ranges and needn't reach their ends.
Inputs may be any that keep to these rules, and one draw needn't show every extreme that they name: `clip_lengths`: each row (one group of 640 tokens) sums to 640. In one row, chosen from the seed, slot 0 holds a single clip of 640 tokens and the other slots are 0; every other row has 4 clips of 1 token or more, one of exactly 512. `caption_lengths`: every group has a clip slot whose caption has exactly 128 live tokens, slot 0 in the group of the single clip. `positions`: each token's index within its clip.
All inputs are finite; a program needn't handle non-finite values.
Results may differ from the reference program's by a relative error of at most 0.013.
Values may be sent and summed in bfloat16 or wider, within the bound.
A program may use at most 448 MiB of HBM per device.

```python
import math
import jax
import jax.numpy as jnp
from jax import lax

D = 1536
H = 24
HD = 64
FF = 4096
TEXT = 4096
TOK_DEV = 160
CPG = 4
CAP = 128
QBLOCK = 640
SEQ = 640
CLIP_MOST = 512
CLIPS = 32
TOKENS = 5120
N_FSDP = 8
N_SP = 4


def clip_table(key):
    seq_len = N_SP * TOK_DEV
    rest = seq_len - CLIP_MOST
    extra = rest - (CPG - 1)
    key_long, key_weight, key_slot = jax.random.split(key, 3)
    long_group = jax.random.randint(key_long, (), 0, N_FSDP)
    weights = jax.random.randint(key_weight, (N_FSDP, CPG - 1), 1, 10)
    whole_weight = jnp.sum(weights, axis=1, keepdims=True)
    pieces = 1 + extra * weights // whole_weight
    first = pieces[:, :CPG - 2]
    final = rest - jnp.sum(first, axis=1, keepdims=True)
    smaller = jnp.concatenate([first, final], axis=1)
    slot = jax.random.randint(key_slot, (N_FSDP, 1), 0, CPG)
    column = jnp.arange(CPG, dtype=jnp.int32)[None, :]
    index = jnp.clip(column - (column > slot).astype(jnp.int32), 0, CPG - 2)
    picked = jnp.take_along_axis(smaller, index, axis=1)
    several = jnp.where(column == slot, CLIP_MOST, picked)
    single = jnp.where(column == 0, seq_len, 0)
    is_single = jnp.arange(N_FSDP)[:, None] == long_group
    return jnp.where(is_single, single, several).astype(jnp.int32)


def draw_clip_lengths(key, part):
    return clip_table(jax.random.fold_in(key, 7))


def draw_positions(key, part):
    table = clip_table(jax.random.fold_in(key, 7))
    seq_len = N_SP * TOK_DEV
    ends = jnp.cumsum(table, axis=1).astype(jnp.int32)
    starts = ends - table
    place = jnp.arange(seq_len, dtype=jnp.int32)
    clip_of = jnp.sum((place[None, :, None] >= ends[:, None, :]).astype(jnp.int32), axis=2)
    begin = jnp.sum(jnp.where(clip_of[:, :, None] == jnp.arange(CPG, dtype=jnp.int32)[None, None, :], starts[:, None, :], 0), axis=2)
    return (place[None, :] - begin).reshape(-1).astype(jnp.int32)


def draw_caption_lengths(key, part):
    table = clip_table(jax.random.fold_in(key, 7))
    key_length, key_slot = jax.random.split(jax.random.fold_in(key, 13))
    lengths = jax.random.randint(key_length, (N_FSDP, CPG), 1, CAP + 1)
    slot = jax.random.randint(key_slot, (N_FSDP, 1), 0, CPG)
    slot = jnp.where(table[:, 1:2] == 0, 0, slot)
    column = jnp.arange(CPG, dtype=jnp.int32)[None, :]
    return jnp.where(column == slot, CAP, lengths).reshape(-1).astype(jnp.int32)


def spiked(result, stream_key, source, target, shards_of, factor):
    owner, partner = [(jnp.arange(result.shape[dim]) // (result.shape[dim] // shards_of)).reshape([-1 if axis == dim else 1 for axis in range(result.ndim)]) for dim in (source, target)]
    chosen = jax.random.permutation(stream_key, shards_of)[partner]
    strong = (owner == chosen) | (owner == (partner + shards_of // 2) % shards_of)
    return jnp.where(strong, factor * result, result)


def block_levels(rng, dims, shards, low, top_value):
    def one(axis_at, parts):
        steps = jax.random.uniform(jax.random.fold_in(jax.random.fold_in(rng, 6), axis_at), (parts,), jnp.float32, low / len(shards), top_value / len(shards))
        return jnp.repeat(jnp.exp(steps), dims[axis_at] // parts).reshape((-1,) + (1,) * (len(dims) - axis_at - 1))

    level = one(*shards[0])
    for cut in shards[1:]:
        level = level * one(*cut)
    return level


def noise(stream_key, shape, deviation, bound, cuts=(), held_as=jnp.bfloat16):
    values = jax.random.normal(stream_key, shape, jnp.float32) * deviation
    if len(cuts) > 0:
        values = block_levels(stream_key, shape, cuts, -0.22, 0.18) * values
    return jnp.clip(values, min=-bound, max=bound).astype(held_as)


def gaussian_with(stream_key, shape, spread, limit, cuts, heavy, held_as=jnp.bfloat16):
    drawn = spread * jax.random.normal(stream_key, shape, jnp.float32)
    if cuts:
        drawn = drawn * block_levels(stream_key, shape, cuts, -0.22, 0.18)
    return jnp.clip(spiked(drawn, jax.random.fold_in(stream_key, 3), *heavy), -limit, limit).astype(held_as)


def setup_inputs(seed: int = 0) -> dict:
    key_of = jax.random.split(jax.random.key(seed), 23)
    tokens = gaussian_with(key_of[0], (TOKENS, D), 1.0, 6.0, ((0, 32),), (0, 1, 32, 2.75))
    condition = noise(key_of[1], (CLIPS, D), 1.0, 6.0, ((0, 8),))
    caption = noise(key_of[2], (CLIPS * CAP, TEXT), 1.0, 6.0, ((0, 32),))
    clip_lengths = draw_clip_lengths(jax.random.fold_in(key_of[22], 71), 0)
    caption_lengths = draw_caption_lengths(jax.random.fold_in(key_of[22], 71), 0)
    positions = draw_positions(jax.random.fold_in(key_of[22], 71), 0)
    ada_weight = noise(key_of[6], (D, 6 * D), D ** -0.5, 0.15625, ((0, 32),))
    ada_bias = noise(key_of[7], (6 * D,), 0.5, 3.0, ((0, 32),))
    attention_gain = jnp.clip(1.0 + 0.1 * jax.random.normal(key_of[8], (D,), jnp.float32), 0.5, 1.5).astype(jnp.bfloat16)
    qkv_weight = noise(key_of[9], (D, 3 * D), D ** -0.5, 0.15625, ((0, 32),))
    query_gain = jnp.clip(1.0 + 0.1 * jax.random.normal(key_of[10], (D,), jnp.float32), 0.5, 1.5).astype(jnp.bfloat16)
    key_gain = jnp.clip(1.0 + 0.1 * jax.random.normal(key_of[11], (D,), jnp.float32), 0.5, 1.5).astype(jnp.bfloat16)
    text_key_weight = noise(key_of[12], (TEXT, D), TEXT ** -0.5, 0.09375, ((0, 32),))
    text_key_gain = jnp.clip(1.0 + 0.1 * jax.random.normal(key_of[13], (D,), jnp.float32), 0.5, 1.5).astype(jnp.bfloat16)
    text_value_weight = noise(key_of[14], (TEXT, D), TEXT ** -0.5, 0.09375, ((0, 32),))
    cross_gate = noise(key_of[15], (D,), 1.0, 3.0, ((0, 32),))
    out_weight = noise(key_of[16], (D, D), ((SEQ // 4) ** 0.5 * D ** -0.5), 5.0, ((0, 32),))
    feedforward_gain = jnp.clip(1.0 + 0.1 * jax.random.normal(key_of[17], (D,), jnp.float32), 0.5, 1.5).astype(jnp.bfloat16)
    gate_weight = noise(key_of[18], (D, FF), D ** -0.5, 0.15625, ((0, 32),))
    up_weight = noise(key_of[19], (D, FF), D ** -0.5, 0.15625, ((0, 32),))
    down_weight = noise(key_of[20], (FF, D), FF ** -0.5, 0.09375, ((0, 32),))
    out_grad = noise(key_of[21], (TOKENS, D), 1.0, 6.0, ((0, 32),))
    return {"tokens": tokens, "condition": condition, "caption": caption, "clip_lengths": clip_lengths, "caption_lengths": caption_lengths, "positions": positions, "ada_weight": ada_weight, "ada_bias": ada_bias, "attention_gain": attention_gain, "qkv_weight": qkv_weight, "query_gain": query_gain, "key_gain": key_gain, "text_key_weight": text_key_weight, "text_key_gain": text_key_gain, "text_value_weight": text_value_weight, "cross_gate": cross_gate, "out_weight": out_weight, "feedforward_gain": feedforward_gain, "gate_weight": gate_weight, "up_weight": up_weight, "down_weight": down_weight, "out_grad": out_grad}


@jax.custom_vjp
def low(v):
    return lax.optimization_barrier(v.astype(jnp.bfloat16)).astype(jnp.float32)

@jax.custom_vjp
def low_back(v):
    return v

def low_keep(v):
    return (low(v), None)

def low_pass(kept, grad):
    return (grad,)

def back_keep(v):
    return (v, None)

def back_low(kept, grad):
    return (low(grad),)
low.defvjp(low_keep, low_pass)
low_back.defvjp(back_keep, back_low)
HIGHEST = lax.Precision.HIGHEST
EPSILON = 1e-06
NEGATIVE = -1e+30

def matmul_high(left, right):
    return jnp.dot(left, right, precision=HIGHEST, preferred_element_type=jnp.float32)

def rms_gain(values, gain):
    return values * lax.rsqrt(lax.optimization_barrier(jnp.mean(values * values, axis=-1, keepdims=True)) + EPSILON) * gain

def norm_modulate(values, gain, scale, shift):
    return rms_gain(values, gain) * (1.0 + scale) + shift

def rope_angles(positions, half):
    freqs = jnp.exp(jnp.arange(half, dtype=jnp.float32) * (-math.log(10000.0) / half))
    return positions.astype(jnp.float32)[:, None] * freqs[None, :]

def rotate(values, angles):
    half = values.shape[-1] // 2
    cosine = jnp.cos(angles)[:, None, :]
    sine = jnp.sin(angles)[:, None, :]
    first = values[..., :half]
    second = values[..., half:]
    return jnp.concatenate([first * cosine - second * sine, first * sine + second * cosine], axis=-1)

def query_key(angles, q_raw, k_raw, query_gain, key_gain):
    rows = q_raw.shape[0]
    query_rot = rotate(rms_gain(q_raw, query_gain).reshape(rows, -1, HD), angles)
    key_rot = rotate(rms_gain(k_raw, key_gain).reshape(rows, -1, HD), angles)
    return (query_rot, key_rot)

def clip_ids(lengths, total):
    ends = jnp.cumsum(lengths).astype(jnp.int32)
    place = jnp.arange(total, dtype=jnp.int32)
    return lax.optimization_barrier(jnp.sum((place[:, None] >= ends[None, :]).astype(jnp.int32), axis=1)).astype(jnp.int32)

def softmax_rows(scores):
    top = lax.optimization_barrier(jnp.max(scores, axis=-1, keepdims=True))
    expo = jnp.exp(scores - top)
    return expo / lax.optimization_barrier(jnp.sum(expo, axis=-1, keepdims=True))

def attend(query, key, value, text_key, text_value, group_clip, caption_clip, caption_live, gate_tanh):
    scale = HD ** (-0.5)
    seq_len = query.shape[0]

    def one_block(begin):
        query_block = lax.dynamic_slice_in_dim(query, begin, QBLOCK)
        clip_block = lax.dynamic_slice_in_dim(group_clip, begin, QBLOCK)
        self_scores = low_back(jnp.einsum('qhd,khd->hqk', query_block, key, precision=HIGHEST) * scale)
        same_clip = (clip_block[:, None] == group_clip[None, :])[None]
        self_prob = low(softmax_rows(jnp.where(same_clip, self_scores, NEGATIVE)))
        self_out = jnp.einsum('hqk,khd->qhd', self_prob, value, precision=HIGHEST)
        cross_scores = low_back(jnp.einsum('qhd,khd->hqk', query_block, text_key, precision=HIGHEST) * scale)
        cross_ok = ((clip_block[:, None] == caption_clip[None, :]) & caption_live[None, :])[None]
        cross_prob = low(softmax_rows(jnp.where(cross_ok, cross_scores, NEGATIVE)))
        cross_out = low_back(jnp.einsum('hqk,khd->qhd', cross_prob, text_value, precision=HIGHEST))
        return self_out + gate_tanh[None] * cross_out
    starts = jnp.arange(seq_len // QBLOCK, dtype=jnp.int32) * QBLOCK
    blocks = lax.map(jax.checkpoint(one_block), starts)
    return blocks.reshape(seq_len, -1)

def group_layer(params, group):
    ada_weight, ada_bias, attention_gain, qkv_weight, query_gain, key_gain, text_key_weight, text_key_gain, text_value_weight, cross_gate, out_weight, feedforward_gain, gate_weight, up_weight, down_weight = params
    tokens, condition, caption, clip_lengths, caption_lengths, positions = group
    seq_len = N_SP * TOK_DEV
    silu_cond = low(jax.nn.silu(condition))
    modulation = matmul_high(silu_cond, ada_weight) + ada_bias
    group_clip = clip_ids(clip_lengths, seq_len)
    one_hot = (group_clip[:, None] == jnp.arange(CPG, dtype=jnp.int32)[None, :]).astype(jnp.float32)
    token_mod = matmul_high(one_hot, modulation)
    shift_one, scale_one, gate_one, shift_two, scale_two, gate_two = jnp.split(token_mod, 6, axis=1)
    normed_one = low(norm_modulate(tokens, attention_gain, scale_one, shift_one))
    projected = low_back(matmul_high(normed_one, qkv_weight))
    q_raw, k_raw, v_raw = jnp.split(projected, 3, axis=1)
    angles = rope_angles(positions, HD // 2)
    query_rot, key_rot = query_key(angles, q_raw, k_raw, query_gain, key_gain)
    query = low(low_back(query_rot))
    key = low(low_back(key_rot))
    value = low(low_back(v_raw)).reshape(seq_len, H, HD)
    text_key_raw = low_back(matmul_high(caption, text_key_weight))
    text_key = low(low_back(rms_gain(text_key_raw, text_key_gain))).reshape(-1, H, HD)
    text_value = low(low_back(matmul_high(caption, text_value_weight))).reshape(-1, H, HD)
    caption_row = jnp.arange(CPG * CAP, dtype=jnp.int32)
    caption_clip = (caption_row // CAP).astype(jnp.int32)
    caption_limit = lax.optimization_barrier(jnp.sum(jnp.where(caption_clip[:, None] == jnp.arange(CPG, dtype=jnp.int32)[None, :], caption_lengths[None, :], 0), axis=1))
    caption_live = caption_row % CAP < caption_limit
    gate_tanh = jnp.tanh(cross_gate).reshape(H, HD)
    mixed = low(low_back(attend(query, key, value, text_key, text_value, group_clip, caption_clip, caption_live, gate_tanh)))
    attended = low_back(matmul_high(mixed, out_weight))
    middle = tokens + gate_one * attended
    normed_two = low(norm_modulate(middle, feedforward_gain, scale_two, shift_two))
    gate_act = low_back(matmul_high(normed_two, gate_weight))
    up_act = low_back(matmul_high(normed_two, up_weight))
    hidden = low(jax.nn.silu(gate_act) * up_act)
    ffn_out = low_back(matmul_high(hidden, down_weight))
    return middle + gate_two * ffn_out

def reference(tokens, condition, caption, clip_lengths, caption_lengths, positions, ada_weight, ada_bias, attention_gain, qkv_weight, query_gain, key_gain, text_key_weight, text_key_gain, text_value_weight, cross_gate, out_weight, feedforward_gain, gate_weight, up_weight, down_weight, out_grad):
    seq_len = N_SP * TOK_DEV
    params = tuple((weight.astype(jnp.float32) for weight in (ada_weight, ada_bias, attention_gain, qkv_weight, query_gain, key_gain, text_key_weight, text_key_gain, text_value_weight, cross_gate, out_weight, feedforward_gain, gate_weight, up_weight, down_weight)))
    inputs = (condition.astype(jnp.float32).reshape(N_FSDP, CPG, D), caption.astype(jnp.float32).reshape(N_FSDP, CPG * CAP, TEXT), clip_lengths.astype(jnp.int32), caption_lengths.astype(jnp.int32).reshape(N_FSDP, CPG), positions.astype(jnp.int32).reshape(N_FSDP, seq_len))

    def whole(token_values, *param_values):

        def scan_step(carry, group):
            return (carry, group_layer(param_values, group))
        unused, outputs = lax.scan(scan_step, jnp.zeros((), jnp.float32), (token_values.reshape(N_FSDP, seq_len, D),) + inputs)
        return outputs.reshape(N_FSDP * seq_len, D)
    output, pullback = jax.vjp(whole, tokens.astype(jnp.float32), *params)
    grads = pullback(out_grad.astype(jnp.float32))
    return (output.astype(jnp.bfloat16), grads[0], grads[1], grads[2], grads[3], grads[4], grads[5], grads[6], grads[7], grads[8], grads[9], grads[10], grads[11], grads[12], grads[13], grads[14], grads[15])
```

```python
import math

import jax
import jax.numpy as jnp
from jax import lax
from jax.sharding import PartitionSpec as P

H = 24
HD = 64
CPG = 4
CAP = 128

HIGHEST = lax.Precision.HIGHEST
EPSILON = 1e-06
NEGATIVE = -1e30
BF16 = jnp.bfloat16
F32 = jnp.float32
ALL = ("fsdp", "sp")


def norm_modulate(values, gain, scale, shift):
    root = lax.rsqrt(jnp.mean(values * values, axis=-1, keepdims=True) + EPSILON)
    return values * root * gain * (1.0 + scale) + shift


def partner(values):
    half = HD // 2
    width = values.shape[1]
    column = lax.broadcasted_iota(jnp.int32, values.shape, 1) % HD
    ahead = jnp.concatenate([values[:, half:], values[:, :half]], axis=1)
    behind = jnp.concatenate([values[:, width - half :], values[:, : width - half]], axis=1)
    return jnp.where(column < half, ahead, behind)


def softmax_rows(scores):
    top = jnp.max(scores, axis=-1, keepdims=True)
    expo = jnp.exp(scores - top)
    return expo / jnp.sum(expo, axis=-1, keepdims=True)


def product(left, right):
    return jnp.dot(left, right, preferred_element_type=F32)


def left_product(left, right):
    return lax.dot_general(left, right, (((0,), (0,)), ((), ())), preferred_element_type=F32)


def right_product(left, right):
    return lax.dot_general(left, right, (((1,), (1,)), ((), ())), preferred_element_type=F32)


def gather(values, axes):
    return lax.all_gather(values, axes, axis=0, tiled=True)


def scatter(values, axes):
    return lax.psum_scatter(values, axes, scatter_dimension=0, tiled=True)


def exchange(values):
    return lax.all_to_all(values, "sp", split_axis=0, concat_axis=0, tiled=True)


def small_sum(values):
    return jnp.sum(lax.all_gather(values, "sp", axis=0), axis=0)


def body(
    tokens,
    condition,
    caption,
    clip_lengths,
    caption_lengths,
    positions,
    ada_weight,
    ada_bias,
    attention_gain,
    qkv_weight,
    query_gain,
    key_gain,
    text_key_weight,
    text_key_gain,
    text_value_weight,
    cross_gate,
    out_weight,
    feedforward_gain,
    gate_weight,
    up_weight,
    down_weight,
    out_grad,
):
    sp = lax.axis_size("sp")
    fsdp = lax.axis_size("fsdp")
    sp_place = lax.axis_index("sp")
    place = lax.axis_index("fsdp") * sp + sp_place
    rows, dim = tokens.shape
    seq = sp * rows
    heads = H // sp
    local = heads * HD
    wrows = qkv_weight.shape[0]
    hidden_dim = gate_weight.shape[1]
    hcols = hidden_dim // (fsdp * sp)
    hlocal = hidden_dim // sp
    text_dim = caption.shape[1]
    tcols = text_dim // (fsdp * sp)
    caps = caption.shape[0] * sp
    bias_rows = ada_bias.shape[0]

    ada_part = gather(ada_weight, "fsdp")
    small = jnp.concatenate(
        [
            ada_bias,
            attention_gain,
            query_gain,
            key_gain,
            text_key_gain,
            cross_gate,
            feedforward_gain,
        ]
    )
    small_all = gather(small[None], ALL).astype(F32)
    bias_full = small_all[:, :bias_rows].reshape(-1)
    gains_full = [
        small_all[:, bias_rows + k * wrows : bias_rows + (k + 1) * wrows].reshape(-1)
        for k in range(6)
    ]
    attention_full, query_full, key_full, text_full, cross_full, feedforward_full = gains_full
    mine = lambda vector: lax.dynamic_slice_in_dim(vector, sp_place * local, local)[None]
    query_mine, key_mine, text_mine = mine(query_full), mine(key_full), mine(text_full)
    gate_tanh = jnp.tanh(mine(cross_full))

    qkv_cols = exchange(
        qkv_weight.reshape(wrows, 3, sp, local)
        .transpose(2, 0, 1, 3)
        .reshape(sp * wrows, 3 * local)
    )
    qkv_full = gather(qkv_cols, "fsdp")
    spread = lambda weight: (
        weight.reshape(wrows, fsdp, sp, hcols)
        .transpose(2, 0, 1, 3)
        .reshape(sp * wrows, hlocal)
    )
    gate_up_cols = exchange(jnp.concatenate([spread(gate_weight), spread(up_weight)], axis=1))
    text_cols = jnp.concatenate(
        [
            text_key_weight.reshape(tcols, sp, 1, local),
            text_value_weight.reshape(tcols, sp, 1, local),
        ],
        axis=2,
    ).reshape(tcols, 2 * dim)
    text_full_weight = gather(text_cols, "fsdp")
    out_full = gather(out_weight, ALL)
    gate_up_full = gather(gate_up_cols, "fsdp")
    gate_full, up_full = gate_up_full[:, :hlocal], gate_up_full[:, hlocal:]
    down_full = gather(down_weight, "fsdp")

    silu_cond = jax.nn.silu(condition.astype(F32)).astype(BF16)
    cond_mine = lax.dynamic_index_in_dim(
        silu_cond.reshape(CPG, fsdp, sp, wrows), sp_place, axis=2, keepdims=False
    ).reshape(CPG, fsdp * wrows)
    modulation = small_sum(product(cond_mine, ada_part)) + bias_full[None]

    lengths = clip_lengths[0]
    ends = jnp.cumsum(lengths)
    token = jnp.arange(seq, dtype=jnp.int32)
    group_clip = jnp.sum((token[:, None] >= ends[None, :]).astype(jnp.int32), axis=1)
    slot = jnp.arange(CPG, dtype=jnp.int32)[None, :]
    group_hot = group_clip[:, None] == slot
    group_place = token - jnp.sum(jnp.where(group_hot, (ends - lengths)[None, :], 0), axis=1)
    token_clip = lax.dynamic_slice_in_dim(group_clip, sp_place * rows, rows)
    one_hot = (token_clip[:, None] == slot).astype(F32)

    def token_mod(k):
        piece = modulation[:, k * dim : (k + 1) * dim]
        value = piece[0:1]
        for c in range(1, CPG):
            value = jnp.where(token_clip[:, None] == c, piece[c : c + 1], value)
        return value

    shift_one, scale_one, gate_one, shift_two, scale_two, gate_two = [
        token_mod(k) for k in range(6)
    ]

    values = tokens.astype(F32)
    normed_one = norm_modulate(values, attention_full[None], scale_one, shift_one).astype(BF16)
    normed_one_all = gather(normed_one, "sp")
    projected = product(normed_one_all, qkv_full)
    q_raw, k_raw, v_raw = (
        projected[:, :local],
        projected[:, local : 2 * local],
        projected[:, 2 * local :],
    )
    qk_squares = small_sum(
        jnp.stack([jnp.sum(q_raw * q_raw, axis=1), jnp.sum(k_raw * k_raw, axis=1)])
    )
    q_root = lax.rsqrt(qk_squares[0] / dim + EPSILON)[:, None]
    k_root = lax.rsqrt(qk_squares[1] / dim + EPSILON)[:, None]
    half = HD // 2
    freqs = jnp.exp(jnp.arange(half, dtype=F32) * (-math.log(10000.0) / half))
    angles = group_place.astype(F32)[:, None] * freqs[None, :]
    cosine = jnp.tile(jnp.cos(angles), (1, 2 * heads))
    sine_half = jnp.sin(angles)
    sine = jnp.tile(jnp.concatenate([-sine_half, sine_half], axis=1), (1, heads))
    rotate = lambda v: v * cosine + partner(v) * sine
    rotate_back = lambda v: v * cosine - partner(v) * sine
    split_heads = lambda v: v.reshape(v.shape[0], heads, HD)
    query = split_heads(rotate(q_raw * q_root * query_mine).astype(BF16))
    key = split_heads(rotate(k_raw * k_root * key_mine).astype(BF16))
    value = split_heads(v_raw.astype(BF16))

    caption_cols = exchange(
        caption.reshape(caption.shape[0], fsdp, sp, tcols)
        .transpose(2, 0, 1, 3)
        .reshape(caps, fsdp * tcols)
    )
    text_parts = jnp.concatenate(
        [
            product(caption_cols, text_full_weight[:, 2 * local * c : 2 * local * (c + 1)]).astype(
                BF16
            )
            for c in range(sp)
        ],
        axis=0,
    )
    text_both = scatter(text_parts, "sp").astype(F32)
    tkey_raw = text_both[:, :local]
    tk_root = lax.rsqrt(small_sum(jnp.sum(tkey_raw * tkey_raw, axis=1)) / dim + EPSILON)[:, None]
    tkey = split_heads((tkey_raw * tk_root * text_mine).astype(BF16))
    tvalue = split_heads(text_both[:, local:].astype(BF16))

    scale = HD**-0.5
    caption_row = jnp.arange(caps, dtype=jnp.int32)
    caption_clip = caption_row // CAP
    caption_limit = jnp.sum(
        jnp.where(caption_clip[:, None] == slot, caption_lengths[None, :], 0), axis=1
    )
    caption_live = caption_row % CAP < caption_limit
    same_clip = (group_clip[:, None] == group_clip[None, :])[None]
    cross_ok = ((group_clip[:, None] == caption_clip[None, :]) & caption_live[None, :])[None]
    to_scores = lambda a, b: jnp.einsum("qhd,khd->hqk", a, b, preferred_element_type=F32)
    to_rows = lambda a, b: jnp.einsum("hqk,khd->qhd", a, b, preferred_element_type=F32)
    to_cols = lambda a, b: jnp.einsum("hqk,qhd->khd", a, b, preferred_element_type=F32)
    self_prob = softmax_rows(jnp.where(same_clip, to_scores(query, key) * scale, NEGATIVE))
    cross_prob = softmax_rows(jnp.where(cross_ok, to_scores(query, tkey) * scale, NEGATIVE))
    self_low = self_prob.astype(BF16)
    cross_low = cross_prob.astype(BF16)
    cross_out = to_rows(cross_low, tvalue).reshape(seq, local)
    mixed_heads = (
        to_rows(self_low, value).reshape(seq, local) + gate_tanh * cross_out
    ).astype(BF16)
    mixed = (
        exchange(mixed_heads).reshape(sp, rows, local).transpose(1, 0, 2).reshape(rows, dim)
    )
    attended = product(mixed, out_full)
    middle = values + gate_one * attended

    normed_two = norm_modulate(middle, feedforward_full[None], scale_two, shift_two).astype(BF16)
    normed_two_all = gather(normed_two, "sp")
    grad_top = out_grad.astype(F32)
    grad_ffn_all = gather((gate_two * grad_top).astype(BF16), "sp")
    gate_act = product(normed_two_all, gate_full)
    up_act = product(normed_two_all, up_full)
    sigmoid = jax.nn.sigmoid(gate_act)
    hidden = (gate_act * sigmoid * up_act).astype(BF16)
    grad_hidden = right_product(grad_ffn_all, down_full)
    grad_gate_act = (grad_hidden * up_act * sigmoid * (1.0 + gate_act * (1.0 - sigmoid))).astype(
        BF16
    )
    grad_up_act = (grad_hidden * gate_act * sigmoid).astype(BF16)
    grad_normed_two = scatter(
        (right_product(grad_gate_act, gate_full) + right_product(grad_up_act, up_full)).astype(
            BF16
        ),
        "sp",
    ).astype(F32)
    ffn_out = scatter(product(hidden, down_full).astype(BF16), "sp").astype(F32)
    output = middle + gate_two * ffn_out
    grad_gate_two = grad_top * ffn_out
    gate_up_rows = scatter(
        jnp.concatenate(
            [
                left_product(normed_two_all, grad_gate_act).astype(BF16),
                left_product(normed_two_all, grad_up_act).astype(BF16),
            ],
            axis=1,
        ),
        "fsdp",
    )
    down_shard = scatter(left_product(hidden, grad_ffn_all).astype(BF16), "fsdp").astype(F32)
    gate_up_back = exchange(gate_up_rows).reshape(sp, wrows, 2, fsdp, hcols)
    gate_up_back = gate_up_back.transpose(2, 1, 3, 0, 4).reshape(2, wrows, hidden_dim).astype(F32)

    unused_two, pull_two = jax.vjp(
        norm_modulate, middle, feedforward_full[None], scale_two, shift_two
    )
    grad_middle_norm, feedforward_grad, grad_scale_two, grad_shift_two = pull_two(grad_normed_two)
    grad_middle = grad_top + grad_middle_norm
    grad_gate_one = grad_middle * attended
    grad_attended = (gate_one * grad_middle).astype(BF16)
    out_shard = scatter(left_product(mixed, grad_attended).astype(BF16), ALL).astype(F32)
    grad_mixed = right_product(grad_attended, out_full).astype(BF16)
    grad_flat = exchange(
        grad_mixed.reshape(rows, sp, local).transpose(1, 0, 2).reshape(seq, local)
    )

    grad_heads = split_heads(grad_flat)
    gate_local = (1.0 - gate_tanh * gate_tanh)[0] * jnp.sum(
        grad_flat.astype(F32) * cross_out, axis=0
    )
    cross_grad = split_heads((gate_tanh * grad_flat.astype(F32)).astype(BF16))
    grad_self = to_scores(grad_heads, value)
    score_grad = (
        self_prob * (grad_self - jnp.sum(self_prob * grad_self, axis=-1, keepdims=True))
    ).astype(BF16)
    grad_cross = to_scores(cross_grad, tvalue)
    cscore_grad = (
        cross_prob * (grad_cross - jnp.sum(cross_prob * grad_cross, axis=-1, keepdims=True))
    ).astype(BF16)
    low = lambda v: v.astype(BF16).reshape(v.shape[0], local).astype(F32)
    query_back = low((to_rows(score_grad, key) + to_rows(cscore_grad, tkey)) * scale)
    key_back = low(to_cols(score_grad, query) * scale)
    value_back = to_cols(self_low, grad_heads).astype(BF16).reshape(seq, local)
    tkey_back = low(to_cols(cscore_grad, query) * scale)
    tvalue_back = to_cols(cross_low, cross_grad).astype(BF16).reshape(caps, local)

    query_turn = rotate_back(query_back)
    key_turn = rotate_back(key_back)
    dots = small_sum(
        jnp.concatenate(
            [
                jnp.sum(query_turn * query_mine * q_raw, axis=1),
                jnp.sum(key_turn * key_mine * k_raw, axis=1),
                jnp.sum(tkey_back * text_mine * tkey_raw, axis=1),
            ]
        )
    )[:, None]

    def norm_back(grad, raw, root, gain, dot):
        raw_grad = root * gain * grad - raw * (root * root * root * dot / dim)
        return raw_grad.astype(BF16), jnp.sum(grad * raw * root, axis=0)

    grad_q, query_gain_grad = norm_back(query_turn, q_raw, q_root, query_mine, dots[:seq])
    grad_k, key_gain_grad = norm_back(key_turn, k_raw, k_root, key_mine, dots[seq : 2 * seq])
    grad_tk, text_gain_grad = norm_back(tkey_back, tkey_raw, tk_root, text_mine, dots[2 * seq :])
    grad_projected = jnp.concatenate([grad_q, grad_k, value_back], axis=1)
    grad_normed_one = scatter(
        right_product(grad_projected, qkv_full).astype(BF16), "sp"
    ).astype(F32)
    qkv_rows = scatter(left_product(normed_one_all, grad_projected).astype(BF16), "fsdp")
    qkv_shard = (
        exchange(qkv_rows)
        .reshape(sp, wrows, 3, local)
        .transpose(1, 2, 0, 3)
        .reshape(wrows, 3 * dim)
        .astype(F32)
    )
    text_grads = gather(jnp.concatenate([grad_tk, tvalue_back], axis=1), "sp")
    text_shard = scatter(
        jnp.concatenate(
            [
                left_product(caption_cols, text_grads[c * caps : (c + 1) * caps]).astype(BF16)
                for c in range(sp)
            ],
            axis=1,
        ),
        "fsdp",
    ).reshape(tcols, sp, 2, local)
    text_key_shard = text_shard[:, :, 0].reshape(tcols, dim).astype(F32)
    text_value_shard = text_shard[:, :, 1].reshape(tcols, dim).astype(F32)

    unused_one, pull_one = jax.vjp(
        norm_modulate, values, attention_full[None], scale_one, shift_one
    )
    grad_tokens_norm, attention_grad, grad_scale_one, grad_shift_one = pull_one(grad_normed_one)
    tokens_grad = grad_middle + grad_tokens_norm

    grad_modulation = lax.dot_general(
        one_hot,
        jnp.concatenate(
            [
                grad_shift_one,
                grad_scale_one,
                grad_gate_one,
                grad_shift_two,
                grad_scale_two,
                grad_gate_two,
            ],
            axis=1,
        ),
        (((0,), (0,)), ((), ())),
        precision=HIGHEST,
        preferred_element_type=F32,
    )
    modulation_all = gather(small_sum(grad_modulation), "fsdp")
    cond_all = gather(silu_cond, "fsdp")
    cond_rows = lax.dynamic_slice_in_dim(cond_all, place * wrows, wrows, axis=1)
    ada_shard = lax.dot_general(
        cond_rows.astype(F32),
        modulation_all,
        (((0,), (0,)), ((), ())),
        precision=HIGHEST,
        preferred_element_type=F32,
    )
    bias_shard = lax.dynamic_slice_in_dim(
        jnp.sum(modulation_all, axis=0), place * bias_rows, bias_rows
    )
    spot = lambda vector: lax.dynamic_update_slice_in_dim(
        jnp.zeros((dim,), F32), vector, sp_place * local, 0
    )
    gain_rows = scatter(
        jnp.stack(
            [
                attention_grad[0],
                spot(query_gain_grad),
                spot(key_gain_grad),
                spot(text_gain_grad),
                spot(gate_local),
                feedforward_grad[0],
            ],
            axis=1,
        )
        .reshape(fsdp * sp, wrows * 6),
        ALL,
    ).reshape(wrows, 6)
    (
        attention_shard,
        query_shard,
        key_shard,
        text_gain_shard,
        cross_shard,
        feedforward_shard,
    ) = [gain_rows[:, k] for k in range(6)]
    return (
        output.astype(BF16),
        tokens_grad,
        ada_shard,
        bias_shard,
        attention_shard,
        qkv_shard,
        query_shard,
        key_shard,
        text_key_shard,
        text_gain_shard,
        text_value_shard,
        cross_shard,
        out_shard,
        feedforward_shard,
        gate_up_back[0],
        gate_up_back[1],
        down_shard,
    )


def solution(mesh):
    return jax.shard_map(
        body,
        mesh=mesh,
        in_specs=(
            P(("fsdp", "sp"), None),
            P("fsdp", None),
            P(("fsdp", "sp"), None),
            P("fsdp", None),
            P("fsdp"),
            P(("fsdp", "sp")),
            P(("fsdp", "sp"), None),
            P(("fsdp", "sp")),
            P(("fsdp", "sp")),
            P(("fsdp", "sp"), None),
            P(("fsdp", "sp")),
            P(("fsdp", "sp")),
            P(("fsdp", "sp"), None),
            P(("fsdp", "sp")),
            P(("fsdp", "sp"), None),
            P(("fsdp", "sp")),
            P(("fsdp", "sp"), None),
            P(("fsdp", "sp")),
            P(("fsdp", "sp"), None),
            P(("fsdp", "sp"), None),
            P(("fsdp", "sp"), None),
            P(("fsdp", "sp"), None),
        ),
        out_specs=(
            P(("fsdp", "sp"), None),
            P(("fsdp", "sp"), None),
            P(("fsdp", "sp"), None),
            P(("fsdp", "sp")),
            P(("fsdp", "sp")),
            P(("fsdp", "sp"), None),
            P(("fsdp", "sp")),
            P(("fsdp", "sp")),
            P(("fsdp", "sp"), None),
            P(("fsdp", "sp")),
            P(("fsdp", "sp"), None),
            P(("fsdp", "sp")),
            P(("fsdp", "sp"), None),
            P(("fsdp", "sp")),
            P(("fsdp", "sp"), None),
            P(("fsdp", "sp"), None),
            P(("fsdp", "sp"), None),
        ),
        check_vma=False,
    )
```

```python
import functools
import math

import jax
import jax.numpy as jnp
from jax import lax
from jax.experimental import pallas as pl
from jax.experimental.pallas import tpu as pltpu
from jax.sharding import PartitionSpec as P

H = 24
HD = 64
CPG = 4
CAP = 128

HIGHEST = lax.Precision.HIGHEST
EPSILON = 1e-06
NEGATIVE = -1e30
BF16 = jnp.bfloat16
F32 = jnp.float32


def norm_modulate(values, gain, scale, shift):
    root = lax.rsqrt(jnp.mean(values * values, axis=-1, keepdims=True) + EPSILON)
    return values * root * gain * (1.0 + scale) + shift


def partner(values):
    half = HD // 2
    width = values.shape[1]
    column = lax.broadcasted_iota(jnp.int32, values.shape, 1) % HD
    ahead = jnp.concatenate([values[:, half:], values[:, :half]], axis=1)
    behind = jnp.concatenate([values[:, width - half :], values[:, : width - half]], axis=1)
    return jnp.where(column < half, ahead, behind)


def softmax_rows(scores):
    top = jnp.max(scores, axis=-1, keepdims=True)
    expo = jnp.exp(scores - top)
    return expo / jnp.sum(expo, axis=-1, keepdims=True)


def product(left, right):
    return jnp.dot(left, right, preferred_element_type=F32)


def left_product(left, right):
    return lax.dot_general(left, right, (((0,), (0,)), ((), ())), preferred_element_type=F32)


def right_product(left, right):
    return lax.dot_general(left, right, (((1,), (1,)), ((), ())), preferred_element_type=F32)


def gather(values):
    return lax.all_gather(values, "fsdp", axis=0, tiled=True)


def scatter(values):
    return lax.psum_scatter(values, "fsdp", scatter_dimension=0, tiled=True)


def shift(values, axis, step):
    size = lax.axis_size(axis)
    return lax.ppermute(values, axis, [(k, (k + step) % size) for k in range(size)])


def tie(*values):
    return lax.optimization_barrier(values)


def push_kernel(axis, size, block, spot, values, result, send_sems, receive_sems):
    me = lax.axis_index(axis)
    barrier = pltpu.get_barrier_semaphore()
    for step in range(1, size):
        pl.semaphore_signal(
            barrier,
            inc=1,
            device_id={axis: lax.rem(me + step, size)},
            device_id_type=pl.DeviceIdType.MESH,
        )
    pl.semaphore_wait(barrier, size - 1)

    def copy(step, place):
        to = lax.rem(me + step, size)
        return pltpu.make_async_remote_copy(
            src_ref=values if block is None else values.at[block(to, step)],
            dst_ref=result.at[place],
            send_sem=send_sems.at[step],
            recv_sem=receive_sems.at[step],
            device_id={axis: to},
            device_id_type=pl.DeviceIdType.MESH,
        )

    for step in range(1, size):
        copy(step, spot(me, step)).start()
    result[spot(me, 0)] = values[...] if block is None else values[block(me, 0)]
    for step in range(1, size):
        origin = lax.rem(me + size - step, size)
        copy(step, spot(origin, step)).wait()


def push(values, axis, block, spot, collective):
    size = lax.axis_size(axis)
    shape = values.shape if block is None else values.shape[1:]
    return pl.pallas_call(
        functools.partial(push_kernel, axis, size, block, spot),
        out_shape=jax.ShapeDtypeStruct((size,) + shape, values.dtype),
        in_specs=[pl.BlockSpec(memory_space=pltpu.VMEM)],
        out_specs=pl.BlockSpec(memory_space=pltpu.VMEM),
        scratch_shapes=[
            pltpu.SemaphoreType.DMA((size,)),
            pltpu.SemaphoreType.DMA((size,)),
        ],
        compiler_params=pltpu.CompilerParams(collective_id=collective, has_side_effects=True),
        name="push_%d" % collective,
    )(values)


def push_gather(values, axis, collective):
    return push(values, axis, None, lambda me, step: me, collective)


def push_blocks(stack, axis, collective):
    return push(stack, axis, lambda to, step: to, lambda me, step: me, collective)


def pick(stack, index):
    return lax.dynamic_index_in_dim(stack, index, axis=0, keepdims=False)


def spread(values, axis):
    return [values] + [shift(values, axis, s) for s in range(1, lax.axis_size(axis))]


def send(stack, axis):
    size, place = lax.axis_size(axis), lax.axis_index(axis)
    return [pick(stack, place)] + [
        shift(pick(stack, (place + s) % size), axis, s) for s in range(1, size)
    ]


def send_turned(stack):
    return [stack[0]] + [shift(stack[s], "sp", -s) for s in range(1, lax.axis_size("sp"))]


def ordered(blocks, axis, dimension, ahead=False):
    size, place = lax.axis_size(axis), lax.axis_index(axis)
    stack = jnp.stack(blocks)
    spot = lambda b: (b - place) % size if ahead else (place - b) % size
    return jnp.concatenate([pick(stack, spot(b)) for b in range(size)], axis=dimension)


def gather_turned(values):
    return jnp.concatenate(spread(values, "sp"), axis=0)


def total(blocks):
    result = blocks[0].astype(F32)
    for block in blocks[1:]:
        result = result + block.astype(F32)
    return result


def turned_blocks(values):
    sp = lax.axis_size("sp")
    return send_turned(values.reshape(sp, values.shape[0] // sp, values.shape[1]))


def small_sum(values):
    return total(spread(values, "sp"))


def turned_sums(parts, collective):
    sp = lax.axis_size("sp")
    count = sum(part.shape[0] for part in parts)
    lines = jnp.concatenate(parts).reshape(count // 128, 128)
    blocks = push(lines, "sp", None, lambda me, step: step, collective)
    blocks = [blocks[s].reshape(count) for s in range(sp)]
    results, begin = [], 0
    for part in parts:
        count = part.shape[0]
        results.append(
            total(
                [
                    jnp.roll(block[begin : begin + count], s * (count // sp))
                    for s, block in enumerate(blocks)
                ]
            )
        )
        begin += count
    return results


def body(
    tokens,
    condition,
    caption,
    clip_lengths,
    caption_lengths,
    positions,
    ada_weight,
    ada_bias,
    attention_gain,
    qkv_weight,
    query_gain,
    key_gain,
    text_key_weight,
    text_key_gain,
    text_value_weight,
    cross_gate,
    out_weight,
    feedforward_gain,
    gate_weight,
    up_weight,
    down_weight,
    out_grad,
):
    sp = lax.axis_size("sp")
    fsdp = lax.axis_size("fsdp")
    sp_place = lax.axis_index("sp")
    place = lax.axis_index("fsdp") * sp + sp_place
    rows, dim = tokens.shape
    seq = sp * rows
    heads = H // sp
    local = heads * HD
    wrows = qkv_weight.shape[0]
    hidden_dim = gate_weight.shape[1]
    hcols = hidden_dim // (fsdp * sp)
    hlocal = hidden_dim // sp
    text_dim = caption.shape[1]
    tcols = text_dim // (fsdp * sp)
    caps = caption.shape[0] * sp
    bias_rows = ada_bias.shape[0]

    columns = lambda weight, parts: (
        weight.reshape(weight.shape[0], parts, sp, weight.shape[1] // (parts * sp))
        .transpose(2, 0, 1, 3)
        .reshape(sp, weight.shape[0], weight.shape[1] // sp)
    )
    tokens_all = gather_turned(tokens)
    qkv_full = gather(ordered(send(columns(qkv_weight, 3), "sp"), "sp", 0))
    down_full = gather(down_weight)

    silu_cond = jax.nn.silu(condition.astype(F32)).astype(BF16)
    cond_all = lax.all_gather(silu_cond, "fsdp", axis=0)
    cond_rows = lax.dynamic_slice_in_dim(cond_all, place * wrows, wrows, axis=2)
    small = jnp.concatenate(
        [
            ada_bias,
            attention_gain,
            query_gain,
            key_gain,
            text_key_gain,
            cross_gate,
            feedforward_gain,
        ]
    ).astype(F32)
    small_size = small.shape[0]
    wide = lambda values, width: jnp.pad(values, ((0, 0), (0, width - values.shape[1])))
    rounded = lambda width: -(-width // 128) * 128
    partial = product(cond_rows.reshape(fsdp * CPG, wrows), ada_weight)
    partial = partial.reshape(fsdp, CPG, 6 * dim)
    small_rows = wide(small.reshape(8, small_size // 8), rounded(small_size // 8))
    pieces = jnp.concatenate(
        [
            jnp.concatenate([partial[:, :, : 3 * dim], partial[:, :, 3 * dim :]], axis=1),
            jnp.broadcast_to(small_rows[None], (fsdp,) + small_rows.shape),
        ],
        axis=2,
    )
    arrived = push_blocks(pieces, "fsdp", 0)
    small_group = arrived[:, :, 3 * dim : 3 * dim + small_size // 8].reshape(8, -1)
    group_size = small_group.shape[1]
    bundles = push_gather(
        jnp.concatenate(
            [
                jnp.sum(arrived[:, :, : 3 * dim], axis=0),
                wide(small_group, rounded(group_size)),
            ],
            axis=1,
        ),
        "sp",
        1,
    )
    small_all = (
        bundles[:, :, 3 * dim : 3 * dim + group_size]
        .reshape(sp, fsdp, small_size)
        .transpose(1, 0, 2)
        .reshape(fsdp * sp, small_size)
    )
    bias_full = small_all[:, :bias_rows].reshape(-1)
    gains_full = [
        small_all[:, bias_rows + k * wrows : bias_rows + (k + 1) * wrows].reshape(-1)
        for k in range(6)
    ]
    attention_full, query_full, key_full, text_full, cross_full, feedforward_full = gains_full
    mine = lambda vector: lax.dynamic_slice_in_dim(vector, sp_place * local, local)[None]
    query_mine, key_mine, text_mine = mine(query_full), mine(key_full), mine(text_full)
    gate_tanh = jnp.tanh(mine(cross_full))
    modulation = jnp.sum(bundles[:, :, : 3 * dim], axis=0)
    modulation = jnp.concatenate([modulation[:CPG], modulation[CPG:]], axis=1) + bias_full[None]

    modulation, caption, text_key_weight, text_value_weight = tie(
        modulation, caption, text_key_weight, text_value_weight
    )

    text_full_weight = gather(
        ordered(
            send(
                jnp.concatenate(
                    [columns(text_key_weight, 1), columns(text_value_weight, 1)], axis=2
                ),
                "sp",
            ),
            "sp",
            0,
        )
    )
    first = text_dim // 4
    caption_first = gather_turned(caption[:, :first])

    lengths = clip_lengths[0]
    ends = jnp.cumsum(lengths)
    token = jnp.arange(seq, dtype=jnp.int32)
    token = (sp_place - token // rows) % sp * rows + token % rows
    group_clip = jnp.sum((token[:, None] >= ends[None, :]).astype(jnp.int32), axis=1)
    slot = jnp.arange(CPG, dtype=jnp.int32)[None, :]
    group_hot = group_clip[:, None] == slot
    group_place = token - jnp.sum(jnp.where(group_hot, (ends - lengths)[None, :], 0), axis=1)
    token_clip = group_clip[:rows]
    one_hot = (token_clip[:, None] == slot).astype(F32)

    def token_mod(k, clips):
        piece = modulation[:, k * dim : (k + 1) * dim]
        value = piece[0:1]
        for c in range(1, CPG):
            value = jnp.where(clips[:, None] == c, piece[c : c + 1], value)
        return value

    shift_one, scale_one, gate_one, shift_two, scale_two, gate_two = [
        token_mod(k, token_clip) for k in range(6)
    ]

    values = tokens.astype(F32)
    normed_one_all = norm_modulate(
        tokens_all.astype(F32),
        attention_full[None],
        token_mod(1, group_clip),
        token_mod(0, group_clip),
    ).astype(BF16)
    projected = product(normed_one_all, qkv_full)
    q_raw, k_raw, v_raw = (
        projected[:, :local],
        projected[:, local : 2 * local],
        projected[:, 2 * local :],
    )
    qk_squares = turned_sums([jnp.sum(q_raw * q_raw, axis=1), jnp.sum(k_raw * k_raw, axis=1)], 2)
    *qk_squares, caption_rest, gate_weight, up_weight, out_weight = tie(
        *qk_squares, caption[:, first:], gate_weight, up_weight, out_weight
    )
    out_full = gather(ordered(spread(out_weight, "sp"), "sp", 0))
    gate_up_full = gather(
        ordered(
            send(
                jnp.concatenate([columns(gate_weight, fsdp), columns(up_weight, fsdp)], axis=2),
                "sp",
            ),
            "sp",
            0,
        )
    )
    gate_full, up_full = gate_up_full[:, :hlocal], gate_up_full[:, hlocal:]
    caption_rest = gather_turned(caption_rest)
    q_root = lax.rsqrt(qk_squares[0] / dim + EPSILON)[:, None]
    k_root = lax.rsqrt(qk_squares[1] / dim + EPSILON)[:, None]
    half = HD // 2
    freqs = jnp.exp(jnp.arange(half, dtype=F32) * (-math.log(10000.0) / half))
    angles = group_place.astype(F32)[:, None] * freqs[None, :]
    cosine = jnp.tile(jnp.cos(angles), (1, 2 * heads))
    sine_half = jnp.sin(angles)
    sine = jnp.tile(jnp.concatenate([-sine_half, sine_half], axis=1), (1, heads))
    rotate = lambda v: v * cosine + partner(v) * sine
    rotate_back = lambda v: v * cosine - partner(v) * sine
    split_heads = lambda v: v.reshape(v.shape[0], heads, HD)
    query = split_heads(rotate(q_raw * q_root * query_mine).astype(BF16))
    key = split_heads(rotate(k_raw * k_root * key_mine).astype(BF16))
    value = split_heads(v_raw.astype(BF16))

    text_both = product(caption_first, text_full_weight[:first]) + product(
        caption_rest, text_full_weight[first:]
    )
    tkey_raw = text_both[:, :local]
    (tk_squares,) = turned_sums([jnp.sum(tkey_raw * tkey_raw, axis=1)], 3)
    tk_squares, out_grad_late = tie(tk_squares, out_grad)
    out_grad_all = gather_turned(out_grad_late)
    tk_root = lax.rsqrt(tk_squares / dim + EPSILON)[:, None]
    tkey = split_heads((tkey_raw * tk_root * text_mine).astype(BF16))
    tvalue = split_heads(text_both[:, local:].astype(BF16))

    scale = HD**-0.5
    caption_row = jnp.arange(caps, dtype=jnp.int32)
    caption_row = (sp_place - caption_row // caption.shape[0]) % sp * caption.shape[
        0
    ] + caption_row % caption.shape[0]
    caption_clip = caption_row // CAP
    caption_limit = jnp.sum(
        jnp.where(caption_clip[:, None] == slot, caption_lengths[None, :], 0), axis=1
    )
    caption_live = caption_row % CAP < caption_limit
    same_clip = (group_clip[:, None] == group_clip[None, :])[None]
    cross_ok = ((group_clip[:, None] == caption_clip[None, :]) & caption_live[None, :])[None]
    to_scores = lambda a, b: jnp.einsum("qhd,khd->hqk", a, b, preferred_element_type=F32)
    to_rows = lambda a, b: jnp.einsum("hqk,khd->qhd", a, b, preferred_element_type=F32)
    to_cols = lambda a, b: jnp.einsum("hqk,qhd->khd", a, b, preferred_element_type=F32)
    self_prob = softmax_rows(jnp.where(same_clip, to_scores(query, key) * scale, NEGATIVE))
    cross_prob = softmax_rows(jnp.where(cross_ok, to_scores(query, tkey) * scale, NEGATIVE))
    self_low = self_prob.astype(BF16)
    cross_low = cross_prob.astype(BF16)
    cross_out = to_rows(cross_low, tvalue).reshape(seq, local)
    mixed_heads = (
        to_rows(self_low, value).reshape(seq, local) + gate_tanh * cross_out
    ).astype(BF16)
    mixed = push(
        mixed_heads.reshape(sp, rows, local),
        "sp",
        lambda to, step: (sp - step) % sp,
        lambda me, step: me,
        5,
    )
    mixed = mixed.transpose(1, 0, 2).reshape(rows, dim)
    attended = product(mixed, out_full)
    middle = values + gate_one * attended

    normed_two = norm_modulate(middle, feedforward_full[None], scale_two, shift_two).astype(BF16)
    normed_two_all = gather_turned(normed_two)
    grad_top = out_grad.astype(F32)
    grad_ffn_all = (token_mod(5, group_clip) * out_grad_all.astype(F32)).astype(BF16)
    gate_act = product(normed_two_all, gate_full)
    up_act = product(normed_two_all, up_full)
    sigmoid = jax.nn.sigmoid(gate_act)
    hidden = (gate_act * sigmoid * up_act).astype(BF16)
    grad_hidden = right_product(grad_ffn_all, down_full)
    grad_gate_act = (grad_hidden * up_act * sigmoid * (1.0 + gate_act * (1.0 - sigmoid))).astype(
        BF16
    )
    grad_up_act = (grad_hidden * gate_act * sigmoid).astype(BF16)
    grad_normed_blocks = turned_blocks(
        (right_product(grad_gate_act, gate_full) + right_product(grad_up_act, up_full)).astype(
            BF16
        )
    )
    gate_up_terms = jnp.concatenate(
        [
            left_product(normed_two_all, grad_gate_act).astype(BF16),
            left_product(normed_two_all, grad_up_act).astype(BF16),
        ],
        axis=1,
    )
    down_terms = left_product(hidden, grad_ffn_all).astype(BF16)
    gate_up_rows = scatter(gate_up_terms)
    down_rows = scatter(down_terms)
    *grad_normed_blocks, unused_gate_up, unused_down = tie(
        *grad_normed_blocks, gate_up_terms, down_terms
    )
    grad_normed_two = total(grad_normed_blocks)
    unused_two, pull_two = jax.vjp(
        norm_modulate, middle, feedforward_full[None], scale_two, shift_two
    )
    grad_middle_norm, feedforward_grad, grad_scale_two, grad_shift_two = pull_two(grad_normed_two)
    grad_middle = grad_top + grad_middle_norm
    grad_gate_one = grad_middle * attended
    grad_attended = (gate_one * grad_middle).astype(BF16)
    out_terms = left_product(mixed, grad_attended).astype(BF16)
    out_rows = scatter(out_terms)
    grad_mixed = right_product(grad_attended, out_full).astype(BF16)
    grad_flat = push(
        grad_mixed.reshape(rows, sp, local).transpose(1, 0, 2),
        "sp",
        lambda to, step: to,
        lambda me, step: step,
        6,
    ).reshape(seq, local)

    grad_flat, hidden, unused_out = tie(grad_flat, hidden, out_terms)
    ffn_out = total(turned_blocks(product(hidden, down_full).astype(BF16)))
    output = middle + gate_two * ffn_out
    grad_gate_two = grad_top * ffn_out

    grad_heads = split_heads(grad_flat)
    gate_local = (1.0 - gate_tanh * gate_tanh)[0] * jnp.sum(
        grad_flat.astype(F32) * cross_out, axis=0
    )
    cross_grad = split_heads((gate_tanh * grad_flat.astype(F32)).astype(BF16))
    grad_cross = to_scores(cross_grad, tvalue)
    cscore_grad = (
        cross_prob * (grad_cross - jnp.sum(cross_prob * grad_cross, axis=-1, keepdims=True))
    ).astype(BF16)
    low = lambda v: v.astype(BF16).reshape(v.shape[0], local).astype(F32)
    tkey_back = low(to_cols(cscore_grad, query) * scale)
    tvalue_back = to_cols(cross_low, cross_grad).astype(BF16).reshape(caps, local)
    gate_up_rows, tkey_back, tvalue_back, grad_heads = tie(
        gate_up_rows, tkey_back, tvalue_back, grad_heads
    )
    grad_self = to_scores(grad_heads, value)
    score_grad = (
        self_prob * (grad_self - jnp.sum(self_prob * grad_self, axis=-1, keepdims=True))
    ).astype(BF16)
    query_back = low((to_rows(score_grad, key) + to_rows(cscore_grad, tkey)) * scale)
    key_back = low(to_cols(score_grad, query) * scale)
    value_back = to_cols(self_low, grad_heads).astype(BF16).reshape(seq, local)
    down_rows, query_back, key_back = tie(down_rows, query_back, key_back)
    down_shard = down_rows.astype(F32)
    gate_up_back = [
        block.reshape(wrows, 2, fsdp, 1, hcols)
        for block in send(gate_up_rows.reshape(sp, wrows, 2 * hlocal), "sp")
    ]
    gate_up_back = (
        ordered(gate_up_back, "sp", 3)
        .transpose(1, 0, 2, 3, 4)
        .reshape(2, wrows, hidden_dim)
        .astype(F32)
    )


    query_turn = rotate_back(query_back)
    key_turn = rotate_back(key_back)
    q_dots, k_dots, tk_dots = [
        dot[:, None]
        for dot in turned_sums(
            [
                jnp.sum(query_turn * query_mine * q_raw, axis=1),
                jnp.sum(key_turn * key_mine * k_raw, axis=1),
                jnp.sum(tkey_back * text_mine * tkey_raw, axis=1),
            ],
            4,
        )
    ]

    def norm_back(grad, raw, root, gain, dot):
        raw_grad = root * gain * grad - raw * (root * root * root * dot / dim)
        return raw_grad.astype(BF16), jnp.sum(grad * raw * root, axis=0)

    grad_q, query_gain_grad = norm_back(query_turn, q_raw, q_root, query_mine, q_dots)
    grad_k, key_gain_grad = norm_back(key_turn, k_raw, k_root, key_mine, k_dots)
    grad_tk, text_gain_grad = norm_back(tkey_back, tkey_raw, tk_root, text_mine, tk_dots)
    grad_projected = jnp.concatenate([grad_q, grad_k, value_back], axis=1)
    grad_normed_blocks = turned_blocks(right_product(grad_projected, qkv_full).astype(BF16))
    qkv_terms = left_product(normed_one_all, grad_projected).astype(BF16)
    qkv_rows = scatter(qkv_terms)
    qkv_back = [
        block.reshape(wrows, 3, 1, local)
        for block in send(qkv_rows.reshape(sp, wrows, 3 * local), "sp")
    ]
    qkv_shard = ordered(qkv_back, "sp", 2).reshape(wrows, 3 * dim).astype(F32)
    text_grads = jnp.concatenate([grad_tk, tvalue_back], axis=1)
    text_terms = jnp.concatenate(
        [
            left_product(caption_first, text_grads).astype(BF16),
            left_product(caption_rest, text_grads).astype(BF16),
        ],
        axis=0,
    )
    text_rows = scatter(text_terms)
    *grad_normed_blocks, unused_qkv, unused_text, out_rows = tie(
        *grad_normed_blocks, qkv_terms, text_terms, out_rows
    )
    out_shard = total(send(out_rows.reshape(sp, wrows, dim), "sp"))
    grad_normed_one = total(grad_normed_blocks)
    text_back = [
        block.reshape(tcols, 2, 1, local)
        for block in send(text_rows.reshape(sp, tcols, 2 * local), "sp")
    ]
    text_shard = ordered(text_back, "sp", 2).astype(F32)
    text_key_shard = text_shard[:, 0].reshape(tcols, dim)
    text_value_shard = text_shard[:, 1].reshape(tcols, dim)

    unused_one, pull_one = jax.vjp(
        norm_modulate, values, attention_full[None], scale_one, shift_one
    )
    grad_tokens_norm, attention_grad, grad_scale_one, grad_shift_one = pull_one(grad_normed_one)
    tokens_grad = grad_middle + grad_tokens_norm

    by_clip = lambda grads: lax.dot_general(
        one_hot,
        jnp.concatenate(grads, axis=1),
        (((0,), (0,)), ((), ())),
        precision=HIGHEST,
        preferred_element_type=F32,
    )
    sums = by_clip(
        [
            grad_shift_one,
            grad_scale_one,
            grad_gate_one,
            grad_shift_two,
            grad_scale_two,
            grad_gate_two,
        ]
    )
    gains_wide = jnp.concatenate([attention_grad, feedforward_grad], axis=1).reshape(8, dim // 4)
    gains_heads = jnp.concatenate(
        [query_gain_grad, key_gain_grad, text_gain_grad, gate_local]
    ).reshape(8, local // 2)
    sent = jnp.concatenate(
        [
            jnp.concatenate([sums[:, : 3 * dim], sums[:, 3 * dim :]], axis=0),
            gains_wide,
            wide(gains_heads, rounded(local // 2)),
        ],
        axis=1,
    )
    blocks = push_gather(sent, "sp", 7)
    summed = jnp.sum(blocks[:, :, : 3 * dim + dim // 4], axis=0)
    heads_rows = (
        blocks[:, :, 3 * dim + dim // 4 : 3 * dim + dim // 4 + local // 2]
        .reshape(sp, 4, local)
        .transpose(1, 0, 2)
        .reshape(8, dim // 2)
    )
    gathered = push_gather(jnp.concatenate([summed, heads_rows], axis=1), "fsdp", 8)
    half_one = gathered[:, :CPG, : 3 * dim].reshape(fsdp * CPG, 3 * dim)
    half_two = gathered[:, CPG:, : 3 * dim].reshape(fsdp * CPG, 3 * dim)
    gain_sums = jnp.sum(gathered[:, :, 3 * dim :], axis=0)
    wide_sums = gain_sums[:, : dim // 4].reshape(2, dim)
    heads_sums = gain_sums[:, dim // 4 :].reshape(4, dim)
    cond_flat = cond_rows.reshape(fsdp * CPG, wrows).astype(F32)
    ada_grad = lambda rows_all: lax.dot_general(
        cond_flat,
        rows_all,
        (((0,), (0,)), ((), ())),
        precision=HIGHEST,
        preferred_element_type=F32,
    )
    ada_shard = jnp.concatenate([ada_grad(half_one), ada_grad(half_two)], axis=1)
    bias_shard = lax.dynamic_slice_in_dim(
        jnp.concatenate([jnp.sum(half_one, axis=0), jnp.sum(half_two, axis=0)]),
        place * bias_rows,
        bias_rows,
    )
    own = lambda vector: lax.dynamic_slice_in_dim(vector, place * wrows, wrows)
    attention_shard, feedforward_shard = own(wide_sums[0]), own(wide_sums[1])
    query_shard, key_shard, text_gain_shard, cross_shard = [own(heads_sums[k]) for k in range(4)]
    return (
        output.astype(BF16),
        tokens_grad,
        ada_shard,
        bias_shard,
        attention_shard,
        qkv_shard,
        query_shard,
        key_shard,
        text_key_shard,
        text_gain_shard,
        text_value_shard,
        cross_shard,
        out_shard,
        feedforward_shard,
        gate_up_back[0],
        gate_up_back[1],
        down_shard,
    )


def solution(mesh):
    return jax.shard_map(
        body,
        mesh=mesh,
        in_specs=(
            P(("fsdp", "sp"), None),
            P("fsdp", None),
            P(("fsdp", "sp"), None),
            P("fsdp", None),
            P("fsdp"),
            P(("fsdp", "sp")),
            P(("fsdp", "sp"), None),
            P(("fsdp", "sp")),
            P(("fsdp", "sp")),
            P(("fsdp", "sp"), None),
            P(("fsdp", "sp")),
            P(("fsdp", "sp")),
            P(("fsdp", "sp"), None),
            P(("fsdp", "sp")),
            P(("fsdp", "sp"), None),
            P(("fsdp", "sp")),
            P(("fsdp", "sp"), None),
            P(("fsdp", "sp")),
            P(("fsdp", "sp"), None),
            P(("fsdp", "sp"), None),
            P(("fsdp", "sp"), None),
            P(("fsdp", "sp"), None),
        ),
        out_specs=(
            P(("fsdp", "sp"), None),
            P(("fsdp", "sp"), None),
            P(("fsdp", "sp"), None),
            P(("fsdp", "sp")),
            P(("fsdp", "sp")),
            P(("fsdp", "sp"), None),
            P(("fsdp", "sp")),
            P(("fsdp", "sp")),
            P(("fsdp", "sp"), None),
            P(("fsdp", "sp")),
            P(("fsdp", "sp"), None),
            P(("fsdp", "sp")),
            P(("fsdp", "sp"), None),
            P(("fsdp", "sp")),
            P(("fsdp", "sp"), None),
            P(("fsdp", "sp"), None),
            P(("fsdp", "sp"), None),
        ),
        check_vma=False,
    )
```

```python
import functools
import math

import jax
import jax.numpy as jnp
from jax import lax
from jax.experimental import pallas as pl
from jax.experimental.pallas import tpu as pltpu
from jax.sharding import PartitionSpec as P

H = 24
HD = 64
CPG = 4
CAP = 128

HIGHEST = lax.Precision.HIGHEST
EPSILON = 1e-06
NEGATIVE = -1e30
BF16 = jnp.bfloat16
F32 = jnp.float32
PUSH_BYTES = 50_000_000


def norm_modulate(values, gain, scale, shift):
    root = lax.rsqrt(jnp.mean(values * values, axis=-1, keepdims=True) + EPSILON)
    return values * root * gain * (1.0 + scale) + shift


def partner(values):
    half = HD // 2
    width = values.shape[1]
    column = lax.broadcasted_iota(jnp.int32, values.shape, 1) % HD
    ahead = jnp.concatenate([values[:, half:], values[:, :half]], axis=1)
    behind = jnp.concatenate([values[:, width - half :], values[:, : width - half]], axis=1)
    return jnp.where(column < half, ahead, behind)


def softmax_rows(scores):
    top = jnp.max(scores, axis=-1, keepdims=True)
    expo = jnp.exp(scores - top)
    return expo / jnp.sum(expo, axis=-1, keepdims=True)


def product(left, right):
    return jnp.dot(left, right, preferred_element_type=F32)


def left_product(left, right):
    return lax.dot_general(left, right, (((0,), (0,)), ((), ())), preferred_element_type=F32)


def right_product(left, right):
    return lax.dot_general(left, right, (((1,), (1,)), ((), ())), preferred_element_type=F32)


def gather(values):
    return lax.all_gather(values, "fsdp", axis=0, tiled=True)


def scatter(values):
    return lax.psum_scatter(values, "fsdp", scatter_dimension=0, tiled=True)


def shift(values, axis, step):
    size = lax.axis_size(axis)
    return lax.ppermute(values, axis, [(k, (k + step) % size) for k in range(size)])


def tie(*values):
    return lax.optimization_barrier(values)


def push_kernel(jobs, *refs):
    count = len(jobs)
    sources, results = refs[:count], refs[count : 2 * count]
    send_sems, receive_sems = refs[2 * count : 3 * count], refs[3 * count :]
    sizes = dict((axis, size) for axis, size, block, spot in jobs)
    place = dict((axis, lax.axis_index(axis)) for axis in sizes)
    barrier = pltpu.get_barrier_semaphore()
    for axis, size in sizes.items():
        for step in range(1, size):
            pl.semaphore_signal(
                barrier,
                inc=1,
                device_id={axis: lax.rem(place[axis] + step, size)},
                device_id_type=pl.DeviceIdType.MESH,
            )
    pl.semaphore_wait(barrier, sum(size - 1 for size in sizes.values()))

    def copy(k, step, spot_there):
        axis, size, block, spot = jobs[k]
        to = lax.rem(place[axis] + step, size)
        return pltpu.make_async_remote_copy(
            src_ref=sources[k] if block is None else sources[k].at[block(to, step)],
            dst_ref=results[k].at[spot_there],
            send_sem=send_sems[k].at[step],
            recv_sem=receive_sems[k].at[step],
            device_id={axis: to},
            device_id_type=pl.DeviceIdType.MESH,
        )

    for k, (axis, size, block, spot) in enumerate(jobs):
        for step in range(1, size):
            copy(k, step, spot(place[axis], step)).start()
    for k, (axis, size, block, spot) in enumerate(jobs):
        me = place[axis]
        results[k][spot(me, 0)] = sources[k][...] if block is None else sources[k][block(me, 0)]
    for k, (axis, size, block, spot) in enumerate(jobs):
        for step in range(1, size):
            origin = lax.rem(place[axis] + size - step, size)
            copy(k, step, spot(origin, step)).wait()


def push_many(jobs, collective):
    sizes = [lax.axis_size(axis) for values, axis, block, spot in jobs]
    return pl.pallas_call(
        functools.partial(
            push_kernel,
            [(axis, size, block, spot) for (v, axis, block, spot), size in zip(jobs, sizes)],
        ),
        out_shape=[
            jax.ShapeDtypeStruct(
                (size,) + (values.shape if block is None else values.shape[1:]), values.dtype
            )
            for (values, axis, block, spot), size in zip(jobs, sizes)
        ],
        in_specs=[pl.BlockSpec(memory_space=pltpu.VMEM)] * len(jobs),
        out_specs=[pl.BlockSpec(memory_space=pltpu.VMEM)] * len(jobs),
        scratch_shapes=[pltpu.SemaphoreType.DMA((size,)) for size in sizes] * 2,
        compiler_params=pltpu.CompilerParams(collective_id=collective, has_side_effects=True),
        cost_estimate=pl.CostEstimate(flops=0, bytes_accessed=PUSH_BYTES, transcendentals=0),
        name="push_%d" % collective,
    )(*[values for values, axis, block, spot in jobs])


def push(values, axis, block, spot, collective):
    return push_many([(values, axis, block, spot)], collective)[0]


def to_all(values, axis):
    return (values, axis, None, lambda me, step: me)


def to_each(stack, axis):
    return (stack, axis, lambda to, step: to, lambda me, step: me)


def pick(stack, index):
    return lax.dynamic_index_in_dim(stack, index, axis=0, keepdims=False)


def spread(values, axis):
    return [values] + [shift(values, axis, s) for s in range(1, lax.axis_size(axis))]


def send(stack, axis):
    size, place = lax.axis_size(axis), lax.axis_index(axis)
    return [pick(stack, place)] + [
        shift(pick(stack, (place + s) % size), axis, s) for s in range(1, size)
    ]


def send_turned(stack):
    return [stack[0]] + [shift(stack[s], "sp", -s) for s in range(1, lax.axis_size("sp"))]


def ordered(blocks, axis, dimension, ahead=False):
    size, place = lax.axis_size(axis), lax.axis_index(axis)
    stack = jnp.stack(blocks)
    spot = lambda b: (b - place) % size if ahead else (place - b) % size
    return jnp.concatenate([pick(stack, spot(b)) for b in range(size)], axis=dimension)


def gather_turned(values):
    return jnp.concatenate(spread(values, "sp"), axis=0)


def total(blocks):
    result = blocks[0].astype(F32)
    for block in blocks[1:]:
        result = result + block.astype(F32)
    return result


def turned_blocks(values):
    sp = lax.axis_size("sp")
    return send_turned(values.reshape(sp, values.shape[0] // sp, values.shape[1]))


def small_sum(values):
    return total(spread(values, "sp"))


def row_sums(parts, collective, turned, jobs=()):
    sp = lax.axis_size("sp")
    count = sum(part.shape[0] for part in parts)
    lines = jnp.concatenate(parts).reshape(count // 128, 128)
    blocks, *others = push_many(
        [(lines, "sp", None, lambda me, step: step), *jobs], collective
    )
    blocks = [blocks[s].reshape(count) for s in range(sp)]
    results, begin = [], 0
    for part in parts:
        count = part.shape[0]
        results.append(
            total(
                [
                    jnp.roll(block[begin : begin + count], s * (count // sp) if turned else 0)
                    for s, block in enumerate(blocks)
                ]
            )
        )
        begin += count
    return results, others


def body(
    tokens,
    condition,
    caption,
    clip_lengths,
    caption_lengths,
    positions,
    ada_weight,
    ada_bias,
    attention_gain,
    qkv_weight,
    query_gain,
    key_gain,
    text_key_weight,
    text_key_gain,
    text_value_weight,
    cross_gate,
    out_weight,
    feedforward_gain,
    gate_weight,
    up_weight,
    down_weight,
    out_grad,
):
    sp = lax.axis_size("sp")
    fsdp = lax.axis_size("fsdp")
    sp_place = lax.axis_index("sp")
    place = lax.axis_index("fsdp") * sp + sp_place
    rows, dim = tokens.shape
    seq = sp * rows
    heads = H // sp
    local = heads * HD
    wrows = qkv_weight.shape[0]
    hidden_dim = gate_weight.shape[1]
    hcols = hidden_dim // (fsdp * sp)
    hlocal = hidden_dim // sp
    text_dim = caption.shape[1]
    tcols = text_dim // (fsdp * sp)
    caps = caption.shape[0] * sp
    bias_rows = ada_bias.shape[0]

    columns = lambda weight, parts: (
        weight.reshape(weight.shape[0], parts, sp, weight.shape[1] // (parts * sp))
        .transpose(2, 0, 1, 3)
        .reshape(sp, weight.shape[0], weight.shape[1] // sp)
    )
    qkv_full = gather(ordered(send(columns(qkv_weight, 3), "sp"), "sp", 0))
    down_full = gather(down_weight)

    silu_cond = jax.nn.silu(condition.astype(F32)).astype(BF16)
    cond_all = lax.all_gather(silu_cond, "fsdp", axis=0)
    cond_rows = lax.dynamic_slice_in_dim(cond_all, place * wrows, wrows, axis=2)
    small = jnp.concatenate(
        [
            ada_bias,
            attention_gain,
            query_gain,
            key_gain,
            text_key_gain,
            cross_gate,
            feedforward_gain,
        ]
    ).astype(F32)
    small_size = small.shape[0]
    wide = lambda values, width: jnp.pad(values, ((0, 0), (0, width - values.shape[1])))
    rounded = lambda width: -(-width // 128) * 128
    partial = product(cond_rows.reshape(fsdp * CPG, wrows), ada_weight)
    partial = partial.reshape(fsdp, CPG, 6 * dim)
    small_rows = wide(small.reshape(8, small_size // 8), rounded(small_size // 8))
    pieces = jnp.concatenate(
        [
            jnp.concatenate([partial[:, :, : 3 * dim], partial[:, :, 3 * dim :]], axis=1),
            jnp.broadcast_to(small_rows[None], (fsdp,) + small_rows.shape),
        ],
        axis=2,
    )
    arrived, tokens_all = push_many(
        [
            to_each(pieces, "fsdp"),
            (tokens, "sp", None, lambda me, step: step),
        ],
        0,
    )
    tokens_all = tokens_all.reshape(seq, dim)
    small_group = arrived[:, :, 3 * dim : 3 * dim + small_size // 8].reshape(8, -1)
    group_size = small_group.shape[1]
    bundle = jnp.concatenate(
        [jnp.sum(arrived[:, :, : 3 * dim], axis=0), wide(small_group, rounded(group_size))],
        axis=1,
    )
    (bundles,) = push_many([to_all(bundle, "sp")], 1)
    bundles, down_full, caption = tie(bundles, down_full, caption)
    caption_all = lax.all_gather(caption, "sp", axis=0, tiled=True)
    small_all = (
        bundles[:, :, 3 * dim : 3 * dim + group_size]
        .reshape(sp, fsdp, small_size)
        .transpose(1, 0, 2)
        .reshape(fsdp * sp, small_size)
    )
    bias_full = small_all[:, :bias_rows].reshape(-1)
    gains_full = [
        small_all[:, bias_rows + k * wrows : bias_rows + (k + 1) * wrows].reshape(-1)
        for k in range(6)
    ]
    attention_full, query_full, key_full, text_full, cross_full, feedforward_full = gains_full
    mine = lambda vector: lax.dynamic_slice_in_dim(vector, sp_place * local, local)[None]
    query_mine, key_mine, text_mine = mine(query_full), mine(key_full), mine(text_full)
    gate_tanh = jnp.tanh(mine(cross_full))
    modulation = jnp.sum(bundles[:, :, : 3 * dim], axis=0)
    modulation = jnp.concatenate([modulation[:CPG], modulation[CPG:]], axis=1) + bias_full[None]

    modulation, text_key_weight, text_value_weight = tie(
        modulation, text_key_weight, text_value_weight
    )

    text_full_weight = gather(
        ordered(
            send(
                jnp.concatenate(
                    [columns(text_key_weight, 1), columns(text_value_weight, 1)], axis=2
                ),
                "sp",
            ),
            "sp",
            0,
        )
    )

    lengths = clip_lengths[0]
    ends = jnp.cumsum(lengths)
    token = jnp.arange(seq, dtype=jnp.int32)
    token = (sp_place - token // rows) % sp * rows + token % rows
    group_clip = jnp.sum((token[:, None] >= ends[None, :]).astype(jnp.int32), axis=1)
    slot = jnp.arange(CPG, dtype=jnp.int32)[None, :]
    group_hot = group_clip[:, None] == slot
    group_place = token - jnp.sum(jnp.where(group_hot, (ends - lengths)[None, :], 0), axis=1)
    token_clip = group_clip[:rows]
    one_hot = (token_clip[:, None] == slot).astype(F32)

    def token_mod(k, clips):
        piece = modulation[:, k * dim : (k + 1) * dim]
        value = piece[0:1]
        for c in range(1, CPG):
            value = jnp.where(clips[:, None] == c, piece[c : c + 1], value)
        return value

    shift_one, scale_one, gate_one, shift_two, scale_two, gate_two = [
        token_mod(k, token_clip) for k in range(6)
    ]

    values = tokens.astype(F32)
    normed_one_all = norm_modulate(
        tokens_all.astype(F32),
        attention_full[None],
        token_mod(1, group_clip),
        token_mod(0, group_clip),
    ).astype(BF16)
    projected = product(normed_one_all, qkv_full)
    q_raw, k_raw, v_raw = (
        projected[:, :local],
        projected[:, local : 2 * local],
        projected[:, 2 * local :],
    )
    qk_squares, others = row_sums([jnp.sum(q_raw * q_raw, axis=1), jnp.sum(k_raw * k_raw, axis=1)], 2, True)
    q_root = lax.rsqrt(qk_squares[0] / dim + EPSILON)[:, None]
    k_root = lax.rsqrt(qk_squares[1] / dim + EPSILON)[:, None]
    half = HD // 2
    freqs = jnp.exp(jnp.arange(half, dtype=F32) * (-math.log(10000.0) / half))
    angles = group_place.astype(F32)[:, None] * freqs[None, :]
    cosine = jnp.tile(jnp.cos(angles), (1, 2 * heads))
    sine_half = jnp.sin(angles)
    sine = jnp.tile(jnp.concatenate([-sine_half, sine_half], axis=1), (1, heads))
    rotate = lambda v: v * cosine + partner(v) * sine
    rotate_back = lambda v: v * cosine - partner(v) * sine
    split_heads = lambda v: v.reshape(v.shape[0], heads, HD)
    query = split_heads(rotate(q_raw * q_root * query_mine).astype(BF16))
    key = split_heads(rotate(k_raw * k_root * key_mine).astype(BF16))
    value = split_heads(v_raw.astype(BF16))

    text_both = product(caption_all, text_full_weight)
    tkey_raw = text_both[:, :local]
    (tk_squares,), others = row_sums([jnp.sum(tkey_raw * tkey_raw, axis=1)], 3, False)
    tk_root = lax.rsqrt(tk_squares / dim + EPSILON)[:, None]
    tkey = split_heads((tkey_raw * tk_root * text_mine).astype(BF16))
    tvalue = split_heads(text_both[:, local:].astype(BF16))

    scale = HD**-0.5
    caption_row = jnp.arange(caps, dtype=jnp.int32)
    caption_clip = caption_row // CAP
    caption_limit = jnp.sum(
        jnp.where(caption_clip[:, None] == slot, caption_lengths[None, :], 0), axis=1
    )
    caption_live = caption_row % CAP < caption_limit
    same_clip = (group_clip[:, None] == group_clip[None, :])[None]
    cross_ok = ((group_clip[:, None] == caption_clip[None, :]) & caption_live[None, :])[None]
    to_scores = lambda a, b: jnp.einsum("qhd,khd->hqk", a, b, preferred_element_type=F32)
    to_rows = lambda a, b: jnp.einsum("hqk,khd->qhd", a, b, preferred_element_type=F32)
    to_cols = lambda a, b: jnp.einsum("hqk,qhd->khd", a, b, preferred_element_type=F32)
    self_prob = softmax_rows(jnp.where(same_clip, to_scores(query, key) * scale, NEGATIVE))
    cross_prob = softmax_rows(jnp.where(cross_ok, to_scores(query, tkey) * scale, NEGATIVE))
    self_low = self_prob.astype(BF16)
    cross_low = cross_prob.astype(BF16)
    cross_out = to_rows(cross_low, tvalue).reshape(seq, local)
    self_rows = to_rows(self_low, value).reshape(seq, local)
    self_rows, gate_weight, up_weight, out_weight, out_grad_late = tie(
        self_rows, gate_weight, up_weight, out_weight, out_grad
    )
    out_grad_all = gather_turned(out_grad_late)
    out_full = gather(ordered(spread(out_weight, "sp"), "sp", 0))
    gate_up_full = gather(
        ordered(
            send(
                jnp.concatenate([columns(gate_weight, fsdp), columns(up_weight, fsdp)], axis=2),
                "sp",
            ),
            "sp",
            0,
        )
    )
    mixed_heads = (self_rows + gate_tanh * cross_out).astype(BF16)
    mixed = push(
        mixed_heads.reshape(sp, rows, local),
        "sp",
        lambda to, step: (sp - step) % sp,
        lambda me, step: me,
        5,
    )
    mixed = mixed.transpose(1, 0, 2).reshape(rows, dim)
    attended = product(mixed, out_full)
    middle = values + gate_one * attended

    normed_two = norm_modulate(middle, feedforward_full[None], scale_two, shift_two).astype(BF16)
    normed_two_all = gather_turned(normed_two)
    grad_top = out_grad.astype(F32)
    grad_ffn_all = (token_mod(5, group_clip) * out_grad_all.astype(F32)).astype(BF16)
    gate_up_act = product(normed_two_all, gate_up_full)
    gate_act, up_act = gate_up_act[:, :hlocal], gate_up_act[:, hlocal:]
    sigmoid = jax.nn.sigmoid(gate_act)
    hidden = (gate_act * sigmoid * up_act).astype(BF16)
    grad_hidden = right_product(grad_ffn_all, down_full)
    grad_gate_act = (grad_hidden * up_act * sigmoid * (1.0 + gate_act * (1.0 - sigmoid))).astype(
        BF16
    )
    grad_up_act = (grad_hidden * gate_act * sigmoid).astype(BF16)
    grad_gate_up = jnp.concatenate([grad_gate_act, grad_up_act], axis=1)
    gate_up_terms = left_product(normed_two_all, grad_gate_up).astype(BF16)
    gate_up_terms, grad_gate_up = tie(gate_up_terms, grad_gate_up)
    grad_normed_blocks = push(
        right_product(grad_gate_up, gate_up_full).astype(BF16).reshape(sp, rows, dim),
        "sp",
        lambda to, step: (sp - step) % sp,
        lambda me, step: step,
        10,
    )
    down_terms = left_product(hidden, grad_ffn_all).astype(BF16)
    gate_up_rows = scatter(gate_up_terms)
    down_rows = scatter(down_terms)
    grad_normed_two = jnp.sum(grad_normed_blocks.astype(F32), axis=0)
    unused_two, pull_two = jax.vjp(
        norm_modulate, middle, feedforward_full[None], scale_two, shift_two
    )
    grad_middle_norm, feedforward_grad, grad_scale_two, grad_shift_two = pull_two(grad_normed_two)
    grad_middle = grad_top + grad_middle_norm
    grad_gate_one = grad_middle * attended
    grad_attended = (gate_one * grad_middle).astype(BF16)
    out_terms = left_product(mixed, grad_attended).astype(BF16)
    out_rows = scatter(out_terms)
    grad_mixed = right_product(grad_attended, out_full).astype(BF16)
    grad_flat = push(
        grad_mixed.reshape(rows, sp, local).transpose(1, 0, 2),
        "sp",
        lambda to, step: to,
        lambda me, step: step,
        6,
    ).reshape(seq, local)

    grad_flat, hidden, unused_out = tie(grad_flat, hidden, out_terms)
    ffn_blocks = turned_blocks(product(hidden, down_full).astype(BF16))

    def norm_back(grad, raw, root, gain, dot):
        raw_grad = root * gain * grad - raw * (root * root * root * dot / dim)
        return raw_grad.astype(BF16), jnp.sum(grad * raw * root, axis=0)

    grad_heads = split_heads(grad_flat)
    gate_local = (1.0 - gate_tanh * gate_tanh)[0] * jnp.sum(
        grad_flat.astype(F32) * cross_out, axis=0
    )
    cross_grad = split_heads((gate_tanh * grad_flat.astype(F32)).astype(BF16))
    grad_cross = to_scores(cross_grad, tvalue)
    cscore_grad = (
        cross_prob * (grad_cross - jnp.sum(cross_prob * grad_cross, axis=-1, keepdims=True))
    ).astype(BF16)
    low = lambda v: v.astype(BF16).reshape(v.shape[0], local).astype(F32)
    tkey_back = low(to_cols(cscore_grad, query) * scale)
    tvalue_back = to_cols(cross_low, cross_grad).astype(BF16).reshape(caps, local)
    (tk_dots,), others = row_sums([jnp.sum(tkey_back * text_mine * tkey_raw, axis=1)], 9, False)
    grad_tk, text_gain_grad = norm_back(tkey_back, tkey_raw, tk_root, text_mine, tk_dots[:, None])
    text_grads = jnp.concatenate([grad_tk, tvalue_back], axis=1)
    text_terms = left_product(caption_all, text_grads).astype(BF16)
    text_rows = scatter(text_terms)
    gate_up_rows, grad_heads, cscore_grad, unused_text = tie(
        gate_up_rows, grad_heads, cscore_grad, text_terms
    )
    gate_up_back = send(gate_up_rows.reshape(sp, wrows, 2 * hlocal), "sp")
    grad_self = to_scores(grad_heads, value)
    score_grad = (
        self_prob * (grad_self - jnp.sum(self_prob * grad_self, axis=-1, keepdims=True))
    ).astype(BF16)
    query_back = low((to_rows(score_grad, key) + to_rows(cscore_grad, tkey)) * scale)
    key_back = low(to_cols(score_grad, query) * scale)
    value_back = to_cols(self_low, grad_heads).astype(BF16).reshape(seq, local)
    down_rows, query_back, key_back, *backs = tie(
        down_rows, query_back, key_back, *gate_up_back, *ffn_blocks
    )
    gate_up_back, ffn_blocks = backs[:sp], backs[sp:]
    ffn_out = total(ffn_blocks)
    output = middle + gate_two * ffn_out
    grad_gate_two = grad_top * ffn_out
    down_shard = down_rows.astype(F32)
    gate_up_back = [
        block.reshape(wrows, 2, fsdp, 1, hcols) for block in gate_up_back
    ]
    gate_up_back = (
        ordered(gate_up_back, "sp", 3)
        .transpose(1, 0, 2, 3, 4)
        .reshape(2, wrows, hidden_dim)
        .astype(F32)
    )


    query_turn = rotate_back(query_back)
    key_turn = rotate_back(key_back)
    dots, (out_back,) = row_sums(
        [
            jnp.sum(query_turn * query_mine * q_raw, axis=1),
            jnp.sum(key_turn * key_mine * k_raw, axis=1),
        ],
        4,
        True,
        [to_each(out_rows.reshape(sp, wrows, dim), "sp")],
    )
    q_dots, k_dots = [dot[:, None] for dot in dots]
    out_shard = jnp.sum(out_back.astype(F32), axis=0)

    grad_q, query_gain_grad = norm_back(query_turn, q_raw, q_root, query_mine, q_dots)
    grad_k, key_gain_grad = norm_back(key_turn, k_raw, k_root, key_mine, k_dots)
    grad_projected = jnp.concatenate([grad_q, grad_k, value_back], axis=1)
    grad_normed_terms = right_product(grad_projected, qkv_full).astype(BF16)
    grad_normed_terms, grad_projected = tie(grad_normed_terms, grad_projected)
    grad_normed_blocks = turned_blocks(grad_normed_terms)
    qkv_terms = left_product(normed_one_all, grad_projected).astype(BF16)
    qkv_rows = scatter(qkv_terms)
    *grad_normed_blocks, unused_qkv = tie(*grad_normed_blocks, qkv_terms)
    grad_normed_one = total(grad_normed_blocks)
    unused_one, pull_one = jax.vjp(
        norm_modulate, values, attention_full[None], scale_one, shift_one
    )
    grad_tokens_norm, attention_grad, grad_scale_one, grad_shift_one = pull_one(grad_normed_one)
    tokens_grad = grad_middle + grad_tokens_norm

    by_clip = lambda grads: lax.dot_general(
        one_hot,
        jnp.concatenate(grads, axis=1),
        (((0,), (0,)), ((), ())),
        precision=HIGHEST,
        preferred_element_type=F32,
    )
    sums = by_clip(
        [
            grad_shift_one,
            grad_scale_one,
            grad_gate_one,
            grad_shift_two,
            grad_scale_two,
            grad_gate_two,
        ]
    )
    gains_wide = jnp.concatenate([attention_grad, feedforward_grad], axis=1).reshape(8, dim // 4)
    gains_heads = jnp.concatenate(
        [query_gain_grad, key_gain_grad, text_gain_grad, gate_local]
    ).reshape(8, local // 2)
    sent = jnp.concatenate(
        [
            jnp.concatenate([sums[:, : 3 * dim], sums[:, 3 * dim :]], axis=0),
            gains_wide,
            wide(gains_heads, rounded(local // 2)),
        ],
        axis=1,
    )
    (blocks,) = push_many([to_all(sent, "sp")], 7)
    summed = jnp.sum(blocks[:, :, : 3 * dim + dim // 4], axis=0)
    heads_rows = (
        blocks[:, :, 3 * dim + dim // 4 : 3 * dim + dim // 4 + local // 2]
        .reshape(sp, 4, local)
        .transpose(1, 0, 2)
        .reshape(8, dim // 2)
    )
    gathered, qkv_back, text_back = push_many(
        [
            to_all(jnp.concatenate([summed, heads_rows], axis=1), "fsdp"),
            to_each(qkv_rows.reshape(sp, wrows, 3 * local), "sp"),
            to_each(text_rows.reshape(sp, tcols, 2 * local), "sp"),
        ],
        8,
    )
    qkv_shard = (
        qkv_back.reshape(sp, wrows, 3, local).transpose(1, 2, 0, 3).reshape(wrows, 3 * dim)
    ).astype(F32)
    text_shard = text_back.reshape(sp, tcols, 2, local).transpose(2, 1, 0, 3).astype(F32)
    text_key_shard = text_shard[0].reshape(tcols, dim)
    text_value_shard = text_shard[1].reshape(tcols, dim)
    half_one = gathered[:, :CPG, : 3 * dim].reshape(fsdp * CPG, 3 * dim)
    half_two = gathered[:, CPG:, : 3 * dim].reshape(fsdp * CPG, 3 * dim)
    gain_sums = jnp.sum(gathered[:, :, 3 * dim :], axis=0)
    wide_sums = gain_sums[:, : dim // 4].reshape(2, dim)
    heads_sums = gain_sums[:, dim // 4 :].reshape(4, dim)
    cond_flat = cond_rows.reshape(fsdp * CPG, wrows).astype(F32)
    ada_grad = lambda rows_all: lax.dot_general(
        cond_flat,
        rows_all,
        (((0,), (0,)), ((), ())),
        precision=HIGHEST,
        preferred_element_type=F32,
    )
    ada_shard = jnp.concatenate([ada_grad(half_one), ada_grad(half_two)], axis=1)
    bias_shard = lax.dynamic_slice_in_dim(
        jnp.concatenate([jnp.sum(half_one, axis=0), jnp.sum(half_two, axis=0)]),
        place * bias_rows,
        bias_rows,
    )
    own = lambda vector: lax.dynamic_slice_in_dim(vector, place * wrows, wrows)
    attention_shard, feedforward_shard = own(wide_sums[0]), own(wide_sums[1])
    query_shard, key_shard, text_gain_shard, cross_shard = [own(heads_sums[k]) for k in range(4)]
    return (
        output.astype(BF16),
        tokens_grad,
        ada_shard,
        bias_shard,
        attention_shard,
        qkv_shard,
        query_shard,
        key_shard,
        text_key_shard,
        text_gain_shard,
        text_value_shard,
        cross_shard,
        out_shard,
        feedforward_shard,
        gate_up_back[0],
        gate_up_back[1],
        down_shard,
    )


def solution(mesh):
    return jax.shard_map(
        body,
        mesh=mesh,
        in_specs=(
            P(("fsdp", "sp"), None),
            P("fsdp", None),
            P(("fsdp", "sp"), None),
            P("fsdp", None),
            P("fsdp"),
            P(("fsdp", "sp")),
            P(("fsdp", "sp"), None),
            P(("fsdp", "sp")),
            P(("fsdp", "sp")),
            P(("fsdp", "sp"), None),
            P(("fsdp", "sp")),
            P(("fsdp", "sp")),
            P(("fsdp", "sp"), None),
            P(("fsdp", "sp")),
            P(("fsdp", "sp"), None),
            P(("fsdp", "sp")),
            P(("fsdp", "sp"), None),
            P(("fsdp", "sp")),
            P(("fsdp", "sp"), None),
            P(("fsdp", "sp"), None),
            P(("fsdp", "sp"), None),
            P(("fsdp", "sp"), None),
        ),
        out_specs=(
            P(("fsdp", "sp"), None),
            P(("fsdp", "sp"), None),
            P(("fsdp", "sp"), None),
            P(("fsdp", "sp")),
            P(("fsdp", "sp")),
            P(("fsdp", "sp"), None),
            P(("fsdp", "sp")),
            P(("fsdp", "sp")),
            P(("fsdp", "sp"), None),
            P(("fsdp", "sp")),
            P(("fsdp", "sp"), None),
            P(("fsdp", "sp")),
            P(("fsdp", "sp"), None),
            P(("fsdp", "sp")),
            P(("fsdp", "sp"), None),
            P(("fsdp", "sp"), None),
            P(("fsdp", "sp"), None),
        ),
        check_vma=False,
    )
```

```python
import functools
import math

import jax
import jax.numpy as jnp
from jax import lax
from jax.experimental import pallas as pl
from jax.experimental.pallas import tpu as pltpu
from jax.sharding import PartitionSpec as P

H = 24
HD = 64
CPG = 4
CAP = 128

HIGHEST = lax.Precision.HIGHEST
EPSILON = 1e-06
NEGATIVE = -1e30
BF16 = jnp.bfloat16
F32 = jnp.float32
PUSH_BYTES = 50_000_000


def norm_modulate(values, gain, scale, shift):
    root = lax.rsqrt(jnp.mean(values * values, axis=-1, keepdims=True) + EPSILON)
    return values * root * gain * (1.0 + scale) + shift


def partner(values):
    half = HD // 2
    width = values.shape[1]
    column = lax.broadcasted_iota(jnp.int32, values.shape, 1) % HD
    ahead = jnp.concatenate([values[:, half:], values[:, :half]], axis=1)
    behind = jnp.concatenate([values[:, width - half :], values[:, : width - half]], axis=1)
    return jnp.where(column < half, ahead, behind)


def softmax_rows(scores):
    top = jnp.max(scores, axis=-1, keepdims=True)
    expo = jnp.exp(scores - top)
    return expo / jnp.sum(expo, axis=-1, keepdims=True)


def product(left, right):
    return jnp.dot(left, right, preferred_element_type=F32)


def left_product(left, right):
    return lax.dot_general(left, right, (((0,), (0,)), ((), ())), preferred_element_type=F32)


def right_product(left, right):
    return lax.dot_general(left, right, (((1,), (1,)), ((), ())), preferred_element_type=F32)


def gather(values):
    return lax.all_gather(values, "fsdp", axis=0, tiled=True)


def scatter(values):
    return lax.psum_scatter(values, "fsdp", scatter_dimension=0, tiled=True)


def shift(values, axis, step):
    size = lax.axis_size(axis)
    return lax.ppermute(values, axis, [(k, (k + step) % size) for k in range(size)])


def tie(*values):
    return lax.optimization_barrier(values)


def push_kernel(jobs, *refs):
    count = len(jobs)
    sources, results = refs[:count], refs[count : 2 * count]
    send_sems, receive_sems = refs[2 * count : 3 * count], refs[3 * count :]
    sizes = dict((axis, size) for axis, size, block, spot in jobs)
    place = dict((axis, lax.axis_index(axis)) for axis in sizes)
    barrier = pltpu.get_barrier_semaphore()
    for axis, size in sizes.items():
        for step in range(1, size):
            pl.semaphore_signal(
                barrier,
                inc=1,
                device_id={axis: lax.rem(place[axis] + step, size)},
                device_id_type=pl.DeviceIdType.MESH,
            )
    pl.semaphore_wait(barrier, sum(size - 1 for size in sizes.values()))

    def copy(k, step, spot_there):
        axis, size, block, spot = jobs[k]
        to = lax.rem(place[axis] + step, size)
        return pltpu.make_async_remote_copy(
            src_ref=sources[k] if block is None else sources[k].at[block(to, step)],
            dst_ref=results[k].at[spot_there],
            send_sem=send_sems[k].at[step],
            recv_sem=receive_sems[k].at[step],
            device_id={axis: to},
            device_id_type=pl.DeviceIdType.MESH,
        )

    for k, (axis, size, block, spot) in enumerate(jobs):
        for step in range(1, size):
            copy(k, step, spot(place[axis], step)).start()
    for k, (axis, size, block, spot) in enumerate(jobs):
        me = place[axis]
        results[k][spot(me, 0)] = sources[k][...] if block is None else sources[k][block(me, 0)]
    for k, (axis, size, block, spot) in enumerate(jobs):
        for step in range(1, size):
            origin = lax.rem(place[axis] + size - step, size)
            copy(k, step, spot(origin, step)).wait()


def push_many(jobs, collective):
    sizes = [lax.axis_size(axis) for values, axis, block, spot in jobs]
    return pl.pallas_call(
        functools.partial(
            push_kernel,
            [(axis, size, block, spot) for (v, axis, block, spot), size in zip(jobs, sizes)],
        ),
        out_shape=[
            jax.ShapeDtypeStruct(
                (size,) + (values.shape if block is None else values.shape[1:]), values.dtype
            )
            for (values, axis, block, spot), size in zip(jobs, sizes)
        ],
        in_specs=[pl.BlockSpec(memory_space=pltpu.VMEM)] * len(jobs),
        out_specs=[pl.BlockSpec(memory_space=pltpu.VMEM)] * len(jobs),
        scratch_shapes=[pltpu.SemaphoreType.DMA((size,)) for size in sizes] * 2,
        compiler_params=pltpu.CompilerParams(collective_id=collective, has_side_effects=True),
        cost_estimate=pl.CostEstimate(flops=0, bytes_accessed=PUSH_BYTES, transcendentals=0),
        name="push_%d" % collective,
    )(*[values for values, axis, block, spot in jobs])


def push(values, axis, block, spot, collective):
    return push_many([(values, axis, block, spot)], collective)[0]


def to_all(values, axis):
    return (values, axis, None, lambda me, step: me)


def to_each(stack, axis):
    return (stack, axis, lambda to, step: to, lambda me, step: me)


def pick(stack, index):
    return lax.dynamic_index_in_dim(stack, index, axis=0, keepdims=False)


def spread(values, axis):
    return [values] + [shift(values, axis, s) for s in range(1, lax.axis_size(axis))]


def send(stack, axis):
    size, place = lax.axis_size(axis), lax.axis_index(axis)
    return [pick(stack, place)] + [
        shift(pick(stack, (place + s) % size), axis, s) for s in range(1, size)
    ]


def send_turned(stack):
    return [stack[0]] + [shift(stack[s], "sp", -s) for s in range(1, lax.axis_size("sp"))]


def ordered(blocks, axis, dimension, ahead=False):
    size, place = lax.axis_size(axis), lax.axis_index(axis)
    stack = jnp.stack(blocks)
    spot = lambda b: (b - place) % size if ahead else (place - b) % size
    return jnp.concatenate([pick(stack, spot(b)) for b in range(size)], axis=dimension)


def gather_turned(values):
    return jnp.concatenate(spread(values, "sp"), axis=0)


def total(blocks):
    result = blocks[0].astype(F32)
    for block in blocks[1:]:
        result = result + block.astype(F32)
    return result


def turned_blocks(values):
    sp = lax.axis_size("sp")
    return send_turned(values.reshape(sp, values.shape[0] // sp, values.shape[1]))


def small_sum(values):
    return total(spread(values, "sp"))


def row_sums(parts, collective, turned, jobs=()):
    sp = lax.axis_size("sp")
    count = sum(part.shape[0] for part in parts)
    lines = jnp.concatenate(parts).reshape(count // 128, 128)
    blocks, *others = push_many(
        [(lines, "sp", None, lambda me, step: step), *jobs], collective
    )
    blocks = [blocks[s].reshape(count) for s in range(sp)]
    results, begin = [], 0
    for part in parts:
        count = part.shape[0]
        results.append(
            total(
                [
                    jnp.roll(block[begin : begin + count], s * (count // sp) if turned else 0)
                    for s, block in enumerate(blocks)
                ]
            )
        )
        begin += count
    return results, others


def body(
    tokens,
    condition,
    caption,
    clip_lengths,
    caption_lengths,
    positions,
    ada_weight,
    ada_bias,
    attention_gain,
    qkv_weight,
    query_gain,
    key_gain,
    text_key_weight,
    text_key_gain,
    text_value_weight,
    cross_gate,
    out_weight,
    feedforward_gain,
    gate_weight,
    up_weight,
    down_weight,
    out_grad,
):
    sp = lax.axis_size("sp")
    fsdp = lax.axis_size("fsdp")
    sp_place = lax.axis_index("sp")
    place = lax.axis_index("fsdp") * sp + sp_place
    rows, dim = tokens.shape
    seq = sp * rows
    heads = H // sp
    local = heads * HD
    wrows = qkv_weight.shape[0]
    hidden_dim = gate_weight.shape[1]
    hcols = hidden_dim // (fsdp * sp)
    hlocal = hidden_dim // sp
    text_dim = caption.shape[1]
    tcols = text_dim // (fsdp * sp)
    caps = caption.shape[0] * sp
    bias_rows = ada_bias.shape[0]

    columns = lambda weight, parts: (
        weight.reshape(weight.shape[0], parts, sp, weight.shape[1] // (parts * sp))
        .transpose(2, 0, 1, 3)
        .reshape(sp, weight.shape[0], weight.shape[1] // sp)
    )
    down_full = gather(down_weight)

    silu_cond = jax.nn.silu(condition.astype(F32)).astype(BF16)
    cond_all = lax.all_gather(silu_cond, "fsdp", axis=0)
    cond_all, qkv_weight = tie(cond_all, qkv_weight)
    qkv_full = gather(ordered(send(columns(qkv_weight, 3), "sp"), "sp", 0))
    cond_rows = lax.dynamic_slice_in_dim(cond_all, place * wrows, wrows, axis=2)
    small = jnp.concatenate(
        [
            ada_bias,
            attention_gain,
            query_gain,
            key_gain,
            text_key_gain,
            cross_gate,
            feedforward_gain,
        ]
    ).astype(F32)
    small_size = small.shape[0]
    wide = lambda values, width: jnp.pad(values, ((0, 0), (0, width - values.shape[1])))
    rounded = lambda width: -(-width // 128) * 128
    partial = product(cond_rows.reshape(fsdp * CPG, wrows), ada_weight)
    partial = partial.reshape(fsdp, CPG, 6 * dim)
    small_rows = wide(small.reshape(8, small_size // 8), rounded(small_size // 8))
    pieces = jnp.concatenate(
        [
            jnp.concatenate([partial[:, :, : 3 * dim], partial[:, :, 3 * dim :]], axis=1),
            jnp.broadcast_to(small_rows[None], (fsdp,) + small_rows.shape),
        ],
        axis=2,
    )
    arrived, tokens_all = push_many(
        [
            to_each(pieces, "fsdp"),
            (tokens, "sp", None, lambda me, step: step),
        ],
        0,
    )
    arrived, caption = tie(arrived, caption)
    tokens_all = tokens_all.reshape(seq, dim)
    small_group = arrived[:, :, 3 * dim : 3 * dim + small_size // 8].reshape(8, -1)
    group_size = small_group.shape[1]
    bundle = jnp.concatenate(
        [jnp.sum(arrived[:, :, : 3 * dim], axis=0), wide(small_group, rounded(group_size))],
        axis=1,
    )
    (bundles,) = push_many([to_all(bundle, "sp")], 1)
    bundles, down_full = tie(bundles, down_full)
    caption_all = lax.all_gather(caption, "sp", axis=0, tiled=True)
    small_all = (
        bundles[:, :, 3 * dim : 3 * dim + group_size]
        .reshape(sp, fsdp, small_size)
        .transpose(1, 0, 2)
        .reshape(fsdp * sp, small_size)
    )
    bias_full = small_all[:, :bias_rows].reshape(-1)
    gains_full = [
        small_all[:, bias_rows + k * wrows : bias_rows + (k + 1) * wrows].reshape(-1)
        for k in range(6)
    ]
    attention_full, query_full, key_full, text_full, cross_full, feedforward_full = gains_full
    mine = lambda vector: lax.dynamic_slice_in_dim(vector, sp_place * local, local)[None]
    query_mine, key_mine, text_mine = mine(query_full), mine(key_full), mine(text_full)
    gate_tanh = jnp.tanh(mine(cross_full))
    modulation = jnp.sum(bundles[:, :, : 3 * dim], axis=0)
    modulation = jnp.concatenate([modulation[:CPG], modulation[CPG:]], axis=1) + bias_full[None]

    lengths = clip_lengths[0]
    ends = jnp.cumsum(lengths)
    token = jnp.arange(seq, dtype=jnp.int32)
    token = (sp_place - token // rows) % sp * rows + token % rows
    group_clip = jnp.sum((token[:, None] >= ends[None, :]).astype(jnp.int32), axis=1)
    slot = jnp.arange(CPG, dtype=jnp.int32)[None, :]
    group_hot = group_clip[:, None] == slot
    group_place = token - jnp.sum(jnp.where(group_hot, (ends - lengths)[None, :], 0), axis=1)
    token_clip = group_clip[:rows]
    one_hot = (token_clip[:, None] == slot).astype(F32)

    def token_mod(k, clips):
        piece = modulation[:, k * dim : (k + 1) * dim]
        value = piece[0:1]
        for c in range(1, CPG):
            value = jnp.where(clips[:, None] == c, piece[c : c + 1], value)
        return value

    shift_one, scale_one, gate_one, shift_two, scale_two, gate_two = [
        token_mod(k, token_clip) for k in range(6)
    ]

    values = tokens.astype(F32)
    normed_one_all = norm_modulate(
        tokens_all.astype(F32),
        attention_full[None],
        token_mod(1, group_clip),
        token_mod(0, group_clip),
    ).astype(BF16)
    projected = product(normed_one_all, qkv_full)
    q_raw, k_raw, v_raw = (
        projected[:, :local],
        projected[:, local : 2 * local],
        projected[:, 2 * local :],
    )
    qk_squares, others = row_sums([jnp.sum(q_raw * q_raw, axis=1), jnp.sum(k_raw * k_raw, axis=1)], 2, True)
    *qk_squares, text_key_weight, text_value_weight = tie(
        *qk_squares, text_key_weight, text_value_weight
    )
    text_full_weight = gather(
        ordered(
            send(
                jnp.concatenate(
                    [columns(text_key_weight, 1), columns(text_value_weight, 1)], axis=2
                ),
                "sp",
            ),
            "sp",
            0,
        )
    )
    q_root = lax.rsqrt(qk_squares[0] / dim + EPSILON)[:, None]
    k_root = lax.rsqrt(qk_squares[1] / dim + EPSILON)[:, None]
    half = HD // 2
    freqs = jnp.exp(jnp.arange(half, dtype=F32) * (-math.log(10000.0) / half))
    angles = group_place.astype(F32)[:, None] * freqs[None, :]
    cosine = jnp.tile(jnp.cos(angles), (1, 2 * heads))
    sine_half = jnp.sin(angles)
    sine = jnp.tile(jnp.concatenate([-sine_half, sine_half], axis=1), (1, heads))
    rotate = lambda v: v * cosine + partner(v) * sine
    rotate_back = lambda v: v * cosine - partner(v) * sine
    split_heads = lambda v: v.reshape(v.shape[0], heads, HD)
    query = split_heads(rotate(q_raw * q_root * query_mine).astype(BF16))
    key = split_heads(rotate(k_raw * k_root * key_mine).astype(BF16))
    value = split_heads(v_raw.astype(BF16))

    text_both = product(caption_all, text_full_weight)
    tkey_raw = text_both[:, :local]
    (tk_squares,), others = row_sums([jnp.sum(tkey_raw * tkey_raw, axis=1)], 3, False)
    tk_root = lax.rsqrt(tk_squares / dim + EPSILON)[:, None]
    tkey = split_heads((tkey_raw * tk_root * text_mine).astype(BF16))
    tvalue = split_heads(text_both[:, local:].astype(BF16))

    scale = HD**-0.5
    caption_row = jnp.arange(caps, dtype=jnp.int32)
    caption_clip = caption_row // CAP
    caption_limit = jnp.sum(
        jnp.where(caption_clip[:, None] == slot, caption_lengths[None, :], 0), axis=1
    )
    caption_live = caption_row % CAP < caption_limit
    same_clip = (group_clip[:, None] == group_clip[None, :])[None]
    cross_ok = ((group_clip[:, None] == caption_clip[None, :]) & caption_live[None, :])[None]
    to_scores = lambda a, b: jnp.einsum("qhd,khd->hqk", a, b, preferred_element_type=F32)
    to_rows = lambda a, b: jnp.einsum("hqk,khd->qhd", a, b, preferred_element_type=F32)
    to_cols = lambda a, b: jnp.einsum("hqk,qhd->khd", a, b, preferred_element_type=F32)
    self_prob = softmax_rows(jnp.where(same_clip, to_scores(query, key) * scale, NEGATIVE))
    cross_prob = softmax_rows(jnp.where(cross_ok, to_scores(query, tkey) * scale, NEGATIVE))
    self_low = self_prob.astype(BF16)
    cross_low = cross_prob.astype(BF16)
    cross_out = to_rows(cross_low, tvalue).reshape(seq, local)
    self_rows = to_rows(self_low, value).reshape(seq, local)
    self_rows, gate_weight, up_weight, out_weight, out_grad_late = tie(
        self_rows, gate_weight, up_weight, out_weight, out_grad
    )
    out_grad_all = gather_turned(out_grad_late)
    out_full = gather(ordered(spread(out_weight, "sp"), "sp", 0))
    gate_up_full = gather(
        ordered(
            send(
                jnp.concatenate([columns(gate_weight, fsdp), columns(up_weight, fsdp)], axis=2),
                "sp",
            ),
            "sp",
            0,
        )
    )
    mixed_heads = (self_rows + gate_tanh * cross_out).astype(BF16)
    mixed = push(
        mixed_heads.reshape(sp, rows, local),
        "sp",
        lambda to, step: (sp - step) % sp,
        lambda me, step: me,
        5,
    )
    mixed = mixed.transpose(1, 0, 2).reshape(rows, dim)
    attended = product(mixed, out_full)
    middle = values + gate_one * attended

    normed_two = norm_modulate(middle, feedforward_full[None], scale_two, shift_two).astype(BF16)
    normed_two_all = gather_turned(normed_two)
    grad_top = out_grad.astype(F32)
    grad_ffn_all = (token_mod(5, group_clip) * out_grad_all.astype(F32)).astype(BF16)
    gate_up_act = product(normed_two_all, gate_up_full)
    gate_act, up_act = gate_up_act[:, :hlocal], gate_up_act[:, hlocal:]
    sigmoid = jax.nn.sigmoid(gate_act)
    hidden = (gate_act * sigmoid * up_act).astype(BF16)
    grad_hidden = right_product(grad_ffn_all, down_full)
    grad_gate_act = (grad_hidden * up_act * sigmoid * (1.0 + gate_act * (1.0 - sigmoid))).astype(
        BF16
    )
    grad_up_act = (grad_hidden * gate_act * sigmoid).astype(BF16)
    grad_gate_up = jnp.concatenate([grad_gate_act, grad_up_act], axis=1)
    gate_up_terms = left_product(normed_two_all, grad_gate_up).astype(BF16)
    gate_up_terms, grad_gate_up = tie(gate_up_terms, grad_gate_up)
    grad_normed_blocks = push(
        right_product(grad_gate_up, gate_up_full).astype(BF16).reshape(sp, rows, dim),
        "sp",
        lambda to, step: (sp - step) % sp,
        lambda me, step: step,
        10,
    )
    down_terms = left_product(hidden, grad_ffn_all).astype(BF16)
    gate_up_rows = scatter(gate_up_terms)
    down_rows = scatter(down_terms)
    grad_normed_two = jnp.sum(grad_normed_blocks.astype(F32), axis=0)
    unused_two, pull_two = jax.vjp(
        norm_modulate, middle, feedforward_full[None], scale_two, shift_two
    )
    grad_middle_norm, feedforward_grad, grad_scale_two, grad_shift_two = pull_two(grad_normed_two)
    grad_middle = grad_top + grad_middle_norm
    grad_gate_one = grad_middle * attended
    grad_attended = (gate_one * grad_middle).astype(BF16)
    out_terms = left_product(mixed, grad_attended).astype(BF16)
    out_rows = scatter(out_terms)
    grad_mixed = right_product(grad_attended, out_full).astype(BF16)
    grad_flat = push(
        grad_mixed.reshape(rows, sp, local).transpose(1, 0, 2),
        "sp",
        lambda to, step: to,
        lambda me, step: step,
        6,
    ).reshape(seq, local)

    grad_flat, hidden, unused_out = tie(grad_flat, hidden, out_terms)
    ffn_blocks = turned_blocks(product(hidden, down_full).astype(BF16))

    def norm_back(grad, raw, root, gain, dot):
        raw_grad = root * gain * grad - raw * (root * root * root * dot / dim)
        return raw_grad.astype(BF16), jnp.sum(grad * raw * root, axis=0)

    grad_heads = split_heads(grad_flat)
    gate_local = (1.0 - gate_tanh * gate_tanh)[0] * jnp.sum(
        grad_flat.astype(F32) * cross_out, axis=0
    )
    cross_grad = split_heads((gate_tanh * grad_flat.astype(F32)).astype(BF16))
    grad_cross = to_scores(cross_grad, tvalue)
    cscore_grad = (
        cross_prob * (grad_cross - jnp.sum(cross_prob * grad_cross, axis=-1, keepdims=True))
    ).astype(BF16)
    low = lambda v: v.astype(BF16).reshape(v.shape[0], local).astype(F32)
    tkey_back = low(to_cols(cscore_grad, query) * scale)
    tvalue_back = to_cols(cross_low, cross_grad).astype(BF16).reshape(caps, local)
    (tk_dots,), others = row_sums([jnp.sum(tkey_back * text_mine * tkey_raw, axis=1)], 9, False)
    grad_tk, text_gain_grad = norm_back(tkey_back, tkey_raw, tk_root, text_mine, tk_dots[:, None])
    text_grads = jnp.concatenate([grad_tk, tvalue_back], axis=1)
    text_terms = left_product(caption_all, text_grads).astype(BF16)
    text_rows = scatter(text_terms)
    gate_up_rows, grad_heads, cscore_grad, unused_text = tie(
        gate_up_rows, grad_heads, cscore_grad, text_terms
    )
    gate_up_back = send(gate_up_rows.reshape(sp, wrows, 2 * hlocal), "sp")
    grad_self = to_scores(grad_heads, value)
    score_grad = (
        self_prob * (grad_self - jnp.sum(self_prob * grad_self, axis=-1, keepdims=True))
    ).astype(BF16)
    query_back = low((to_rows(score_grad, key) + to_rows(cscore_grad, tkey)) * scale)
    key_back = low(to_cols(score_grad, query) * scale)
    value_back = to_cols(self_low, grad_heads).astype(BF16).reshape(seq, local)
    down_rows, query_back, key_back, *backs = tie(
        down_rows, query_back, key_back, *gate_up_back, *ffn_blocks
    )
    gate_up_back, ffn_blocks = backs[:sp], backs[sp:]
    ffn_out = total(ffn_blocks)
    output = middle + gate_two * ffn_out
    grad_gate_two = grad_top * ffn_out
    down_shard = down_rows.astype(F32)
    gate_up_back = [
        block.reshape(wrows, 2, fsdp, 1, hcols) for block in gate_up_back
    ]
    gate_up_back = (
        ordered(gate_up_back, "sp", 3)
        .transpose(1, 0, 2, 3, 4)
        .reshape(2, wrows, hidden_dim)
        .astype(F32)
    )


    query_turn = rotate_back(query_back)
    key_turn = rotate_back(key_back)
    dots, (out_back,) = row_sums(
        [
            jnp.sum(query_turn * query_mine * q_raw, axis=1),
            jnp.sum(key_turn * key_mine * k_raw, axis=1),
        ],
        4,
        True,
        [to_each(out_rows.reshape(sp, wrows, dim), "sp")],
    )
    q_dots, k_dots = [dot[:, None] for dot in dots]
    out_shard = jnp.sum(out_back.astype(F32), axis=0)

    grad_q, query_gain_grad = norm_back(query_turn, q_raw, q_root, query_mine, q_dots)
    grad_k, key_gain_grad = norm_back(key_turn, k_raw, k_root, key_mine, k_dots)
    grad_projected = jnp.concatenate([grad_q, grad_k, value_back], axis=1)
    grad_normed_terms = right_product(grad_projected, qkv_full).astype(BF16)
    grad_normed_terms, grad_projected = tie(grad_normed_terms, grad_projected)
    grad_normed_blocks = turned_blocks(grad_normed_terms)
    qkv_terms = left_product(normed_one_all, grad_projected).astype(BF16)
    qkv_rows = scatter(qkv_terms)
    *grad_normed_blocks, unused_qkv = tie(*grad_normed_blocks, qkv_terms)
    grad_normed_one = total(grad_normed_blocks)
    unused_one, pull_one = jax.vjp(
        norm_modulate, values, attention_full[None], scale_one, shift_one
    )
    grad_tokens_norm, attention_grad, grad_scale_one, grad_shift_one = pull_one(grad_normed_one)
    tokens_grad = grad_middle + grad_tokens_norm

    by_clip = lambda grads: lax.dot_general(
        one_hot,
        jnp.concatenate(grads, axis=1),
        (((0,), (0,)), ((), ())),
        precision=HIGHEST,
        preferred_element_type=F32,
    )
    sums = by_clip(
        [
            grad_shift_one,
            grad_scale_one,
            grad_gate_one,
            grad_shift_two,
            grad_scale_two,
            grad_gate_two,
        ]
    )
    gains_wide = jnp.concatenate([attention_grad, feedforward_grad], axis=1).reshape(8, dim // 4)
    gains_heads = jnp.concatenate(
        [query_gain_grad, key_gain_grad, text_gain_grad, gate_local]
    ).reshape(8, local // 2)
    sent = jnp.concatenate(
        [
            jnp.concatenate([sums[:, : 3 * dim], sums[:, 3 * dim :]], axis=0),
            gains_wide,
            wide(gains_heads, rounded(local // 2)),
        ],
        axis=1,
    )
    (blocks,) = push_many([to_all(sent, "sp")], 7)
    summed = jnp.sum(blocks[:, :, : 3 * dim + dim // 4], axis=0)
    heads_rows = (
        blocks[:, :, 3 * dim + dim // 4 : 3 * dim + dim // 4 + local // 2]
        .reshape(sp, 4, local)
        .transpose(1, 0, 2)
        .reshape(8, dim // 2)
    )
    gathered, qkv_back, text_back = push_many(
        [
            to_all(jnp.concatenate([summed, heads_rows], axis=1), "fsdp"),
            to_each(qkv_rows.reshape(sp, wrows, 3 * local), "sp"),
            to_each(text_rows.reshape(sp, tcols, 2 * local), "sp"),
        ],
        8,
    )
    qkv_shard = (
        qkv_back.reshape(sp, wrows, 3, local).transpose(1, 2, 0, 3).reshape(wrows, 3 * dim)
    ).astype(F32)
    text_shard = text_back.reshape(sp, tcols, 2, local).transpose(2, 1, 0, 3).astype(F32)
    text_key_shard = text_shard[0].reshape(tcols, dim)
    text_value_shard = text_shard[1].reshape(tcols, dim)
    half_one = gathered[:, :CPG, : 3 * dim].reshape(fsdp * CPG, 3 * dim)
    half_two = gathered[:, CPG:, : 3 * dim].reshape(fsdp * CPG, 3 * dim)
    gain_sums = jnp.sum(gathered[:, :, 3 * dim :], axis=0)
    wide_sums = gain_sums[:, : dim // 4].reshape(2, dim)
    heads_sums = gain_sums[:, dim // 4 :].reshape(4, dim)
    cond_flat = cond_rows.reshape(fsdp * CPG, wrows).astype(F32)
    ada_grad = lambda rows_all: lax.dot_general(
        cond_flat,
        rows_all,
        (((0,), (0,)), ((), ())),
        precision=HIGHEST,
        preferred_element_type=F32,
    )
    ada_shard = jnp.concatenate([ada_grad(half_one), ada_grad(half_two)], axis=1)
    bias_shard = lax.dynamic_slice_in_dim(
        jnp.concatenate([jnp.sum(half_one, axis=0), jnp.sum(half_two, axis=0)]),
        place * bias_rows,
        bias_rows,
    )
    own = lambda vector: lax.dynamic_slice_in_dim(vector, place * wrows, wrows)
    attention_shard, feedforward_shard = own(wide_sums[0]), own(wide_sums[1])
    query_shard, key_shard, text_gain_shard, cross_shard = [own(heads_sums[k]) for k in range(4)]
    return (
        output.astype(BF16),
        tokens_grad,
        ada_shard,
        bias_shard,
        attention_shard,
        qkv_shard,
        query_shard,
        key_shard,
        text_key_shard,
        text_gain_shard,
        text_value_shard,
        cross_shard,
        out_shard,
        feedforward_shard,
        gate_up_back[0],
        gate_up_back[1],
        down_shard,
    )


def solution(mesh):
    return jax.shard_map(
        body,
        mesh=mesh,
        in_specs=(
            P(("fsdp", "sp"), None),
            P("fsdp", None),
            P(("fsdp", "sp"), None),
            P("fsdp", None),
            P("fsdp"),
            P(("fsdp", "sp")),
            P(("fsdp", "sp"), None),
            P(("fsdp", "sp")),
            P(("fsdp", "sp")),
            P(("fsdp", "sp"), None),
            P(("fsdp", "sp")),
            P(("fsdp", "sp")),
            P(("fsdp", "sp"), None),
            P(("fsdp", "sp")),
            P(("fsdp", "sp"), None),
            P(("fsdp", "sp")),
            P(("fsdp", "sp"), None),
            P(("fsdp", "sp")),
            P(("fsdp", "sp"), None),
            P(("fsdp", "sp"), None),
            P(("fsdp", "sp"), None),
            P(("fsdp", "sp"), None),
        ),
        out_specs=(
            P(("fsdp", "sp"), None),
            P(("fsdp", "sp"), None),
            P(("fsdp", "sp"), None),
            P(("fsdp", "sp")),
            P(("fsdp", "sp")),
            P(("fsdp", "sp"), None),
            P(("fsdp", "sp")),
            P(("fsdp", "sp")),
            P(("fsdp", "sp"), None),
            P(("fsdp", "sp")),
            P(("fsdp", "sp"), None),
            P(("fsdp", "sp")),
            P(("fsdp", "sp"), None),
            P(("fsdp", "sp")),
            P(("fsdp", "sp"), None),
            P(("fsdp", "sp"), None),
            P(("fsdp", "sp"), None),
        ),
        check_vma=False,
    )
```
